32 devices in a mesh: grp: 4 (over z), tile: 8 (over y, x, core).
Axes of the slice: x: 2, y: 2, z: 4, core: 2. Of those that a mesh axis runs over, the one named last changes fastest.
Arguments:
- cotangent: bfloat16 [1, 32, 48, 128, 128], P(None, None, 'grp', 'tile'), may hold values from -6 to 6
- deriv_two: bfloat16 [1, 32, 48, 128, 128], P(None, None, 'grp', 'tile'), may hold values from -0.099609375 to 1.09375
- deriv_one: bfloat16 [1, 32, 48, 128, 128], P(None, None, 'grp', 'tile'), may hold values from -0.099609375 to 1.09375
- point_two: bfloat16 [32, 32], replicated, may hold values from -1 to 1
- point_one: bfloat16 [32, 32], replicated, may hold values from -1 to 1
- modes_two: float32 [1728, 32, 32], P('grp', 'tile'), may hold values from -6 to 6
- modes_one: float32 [1728, 32, 32], P('grp', 'tile'), may hold values from -6 to 6
- saved_two: float32 [1, 1728, 32], P(None, 'grp'), may hold values from -6 to 6
- saved_one: float32 [1, 1728, 32], P(None, 'grp'), may hold values from -6 to 6
Outputs:
- input_grad: bfloat16 [1, 32, 48, 128, 128], P(None, None, 'grp', 'tile')
- grad_one: float32 [1728, 32, 32], P('grp', 'tile')
- grad_two: float32 [1728, 32, 32], P('grp', 'tile')
The draws below stay inside these ranges and needn't reach their ends.
All inputs are finite; a program needn't handle non-finite values.
Results may differ from the reference program's by a relative error of at most 0.01.
Values sent between devices are 32-bit elements; how exact they have to be, the bound alone decides.
No kernel may reach another device: no remote copies, remote signals or barrier semaphores. Data moves between devices by JAX's collectives and lax.ppermute only.
A program may use at most 64 MiB of HBM per device.

```python
import math
import jax
import jax.numpy as jnp
from jax import lax

C = 32
K = 12
SAMPLES = 1
NZ = 128
MODES = 1728
NX = 48
NY = 128


def block_scale(stream_key, extent, cuts, smallest, top_value):
    def one(dim, parts):
        draws = jax.random.uniform(jax.random.fold_in(jax.random.fold_in(stream_key, 6), dim), (parts,), jnp.float32, smallest / len(cuts), top_value / len(cuts))
        return jnp.repeat(jnp.exp(draws), extent[dim] // parts).reshape((-1,) + (1,) * (len(extent) - dim - 1))

    factor_of = one(*cuts[0])
    for cut in cuts[1:]:
        factor_of = factor_of * one(*cut)
    return factor_of


def centred(key, shape, scale, limit, cuts=(), kind=jnp.bfloat16):
    array = jax.random.normal(key, shape, jnp.float32) * scale
    if len(cuts) > 0:
        array = block_scale(key, shape, cuts, -0.22, 0.18) * array
    return jnp.clip(array, min=-limit, max=limit).astype(kind)


def setup_inputs(seed: int = 0) -> dict:
    key_list = jax.random.split(jax.random.key(seed), 10)
    return {
        "cotangent": centred(key_list[0], (SAMPLES, C, NX, NY, NZ), 1.0, 6.0, ((2, 4), (3, 8))),
        "deriv_two": jnp.clip(-0.099609375 + 1.1933594 * jax.random.uniform(key_list[1], (SAMPLES, C, NX, NY, NZ), jnp.float32) ** block_scale(key_list[1], (SAMPLES, C, NX, NY, NZ), ((2, 4), (3, 8)), -0.2, 0.2), -0.099609375, 1.09375).astype(jnp.bfloat16),
        "deriv_one": jnp.clip(-0.099609375 + 1.1933594 * jax.random.uniform(key_list[2], (SAMPLES, C, NX, NY, NZ), jnp.float32) ** block_scale(key_list[2], (SAMPLES, C, NX, NY, NZ), ((2, 4), (3, 8)), -0.2, 0.2), -0.099609375, 1.09375).astype(jnp.bfloat16),
        "point_two": centred(key_list[3], (C, C), C ** -0.5, 1.0),
        "point_one": centred(key_list[4], (C, C), C ** -0.5, 1.0),
        "modes_two": centred(key_list[5], (MODES, C, C), 1.0, 6.0, ((0, 4), (1, 8)), jnp.float32),
        "modes_one": centred(key_list[6], (MODES, C, C), 1.0, 6.0, ((0, 4), (1, 8)), jnp.float32),
        "saved_two": centred(key_list[7], (SAMPLES, MODES, C), 1.0, 6.0, ((1, 4),), jnp.float32),
        "saved_one": centred(key_list[8], (SAMPLES, MODES, C), 1.0, 6.0, ((1, 4),), jnp.float32),
    }


def basis(length, offset, number):
    position = offset + jnp.arange(number, dtype=jnp.int32)
    orders = jnp.arange(K, dtype=jnp.int32)
    frequency = (orders + 1) // 2
    phase = frequency[:, None] * position[None, :] % length
    phase_angle = 2.0 * math.pi / length * phase.astype(jnp.float32)
    factor = math.sqrt(2.0 / length)
    odd_rows = orders[:, None] % 2 == 1
    values = jnp.where(orders[:, None] == 0, jnp.float32(1.0 / math.sqrt(length)), jnp.where(odd_rows, factor * jnp.cos(phase_angle), factor * jnp.sin(phase_angle)))
    return values.astype(jnp.float32)

def layer_backward(upstream, derivative, point_w, mode_w, saved_modes):
    high = lax.Precision.HIGHEST
    table_x = basis(NX, 0, NX)
    table_y = basis(NY, 0, NY)
    table_z = basis(NZ, 0, NZ)
    table_low = lax.optimization_barrier(table_z.astype(jnp.bfloat16)).astype(jnp.float32)
    point_f = point_w.astype(jnp.float32)

    def per_sample(sample_pair):
        field, deriv_field = sample_pair
        gated = (field.astype(jnp.float32) * deriv_field.astype(jnp.float32)).astype(jnp.bfloat16)
        gradient_f = gated.astype(jnp.float32)
        section_one = jnp.einsum('cxyz,kz->cxyk', gradient_f, table_low, precision=high)
        section_two = jnp.einsum('cxyk,by->cxbk', section_one, table_y, precision=high)
        spectrum = jnp.einsum('cxbk,ax->abkc', section_two, table_x, precision=high).reshape(K * K * K, C)
        dual_modes = jnp.einsum('moi,mo->mi', mode_w, spectrum, precision=high)
        dual_grid = dual_modes.reshape(K, K, K, C)
        synth_one = jnp.einsum('abki,ax->ixbk', dual_grid, table_x, precision=high)
        synth_two = jnp.einsum('ixbk,by->ixyk', synth_one, table_y, precision=high)
        synth = jnp.einsum('ixyk,kz->ixyz', synth_two, table_z, precision=high)
        pointwise = jnp.einsum('oi,oxyz->ixyz', point_f, gradient_f, precision=high)
        return ((pointwise + synth).astype(jnp.bfloat16), spectrum)
    result, spectra = lax.map(per_sample, (upstream, derivative))
    weight_grad = jnp.einsum('smo,smi->moi', spectra, saved_modes, precision=high)
    return (result, weight_grad)

def reference(cotangent, deriv_two, deriv_one, point_two, point_one, modes_two, modes_one, saved_two, saved_one):
    middle, grad_two = layer_backward(cotangent, deriv_two, point_two, modes_two, saved_two)
    input_grad, grad_one = layer_backward(middle, deriv_one, point_one, modes_one, saved_one)
    return (input_grad, grad_one, grad_two)
```

```python
import functools
import math

import jax
import jax.numpy as jnp
import numpy as np
from jax import lax
from jax.experimental import pallas as pl
from jax.experimental.pallas import tpu as pltpu
from jax.sharding import PartitionSpec as P

K = 12
LANES = 128
SUB = 8
HIGH = lax.Precision.HIGHEST
BOTH = ("grp", "tile")
VMEM = pl.BlockSpec(memory_space=pltpu.VMEM)
SMEM = pl.BlockSpec(memory_space=pltpu.SMEM)
F32 = jnp.float32
BF16 = jnp.bfloat16


def basis(length):
    position = np.arange(length)
    orders = np.arange(K)
    frequency = (orders + 1) // 2
    phase = frequency[:, None] * position[None, :] % length
    angle = 2.0 * math.pi / length * phase
    factor = math.sqrt(2.0 / length)
    values = np.where(orders[:, None] % 2 == 1, factor * np.cos(angle), factor * np.sin(angle))
    values[0] = 1.0 / math.sqrt(length)
    return values.astype(np.float32)


class Plan:
    def __init__(self, mesh, cells, channels):
        self.groups, self.tiles = mesh.shape["grp"], mesh.shape["tile"]
        self.devices = self.groups * self.tiles
        self.x, self.y, self.z = cells
        self.c = channels
        self.per_row = LANES // channels
        self.blocks = K // self.per_row
        self.width = K * channels
        self.pairs = K * K // self.groups
        self.run = -(-self.pairs // self.tiles)
        self.slot = -(-self.run * self.blocks // SUB) * SUB
        self.packed = self.slot + SUB
        self.rows = self.devices * self.run
        self.own = channels // self.tiles
        self.step = 8

    def valid(self, tile):
        return max(0, min(self.run, self.pairs - self.run * tile))


def call(body, plan, outs, scratch=(), specs=None, name=None, count=None):
    return pl.pallas_call(
        functools.partial(body, plan),
        out_shape=tuple(jax.ShapeDtypeStruct(s, d) for s, d in outs),
        in_specs=specs or [VMEM] * count,
        out_specs=tuple(VMEM for _ in outs),
        scratch_shapes=list(scratch),
        compiler_params=pltpu.CompilerParams(vmem_limit_bytes=48 << 20),
        name=name,
    )


def forward_weights(plan, tz_ref, mask_ref, first):
    table = tz_ref[...]
    parts = []
    for u in range(plan.step):
        parts.append(table * mask_ref[first + u])
    return jnp.concatenate(parts, axis=0)


def emit_slots(plan, acc, ax_ref, by_ref, slots_ref, s_ref):
    p = plan
    s_ref[...] = jnp.dot(ax_ref[...] * by_ref[...], acc, precision=HIGH, preferred_element_type=F32)
    for d in range(p.devices):
        for j in range(p.blocks):
            slots_ref[d, j * p.run : (j + 1) * p.run, :] = s_ref[
                d * p.run : (d + 1) * p.run, j * LANES : (j + 1) * LANES
            ]
        if p.blocks * p.run < p.slot:
            slots_ref[d, p.blocks * p.run :, :] = jnp.zeros((p.slot - p.blocks * p.run, LANES), F32)


def analyse_body(plan, up_ref, der_ref, tz_ref, mask_ref, ax_ref, by_ref, gated_ref, slots_ref, acc_ref, s_ref):
    p = plan
    acc_ref[...] = jnp.zeros_like(acc_ref)

    def group(n, carry):
        first = n * p.step
        weights = forward_weights(p, tz_ref, mask_ref, first)
        parts = []
        for u in range(p.step):
            gated = (up_ref[first + u].astype(F32) * der_ref[first + u].astype(F32)).astype(BF16)
            gated_ref[first + u] = gated
            parts.append(gated)
        acc_ref[...] += jnp.dot(jnp.concatenate(parts, axis=1), weights, preferred_element_type=F32)
        return carry

    lax.fori_loop(0, p.c // p.step, group, 0)
    emit_slots(p, acc_ref[...], ax_ref, by_ref, slots_ref, s_ref)


def gather_modes(plan, got_ref, ax_ref, by_ref, d_ref):
    p = plan
    for d in range(p.devices):
        for j in range(p.blocks):
            d_ref[d * p.run : (d + 1) * p.run, j * LANES : (j + 1) * LANES] = got_ref[
                d, j * p.run : (j + 1) * p.run, :
            ]
    table = ax_ref[...] * by_ref[...]
    return lax.dot_general(
        table, d_ref[...], (((0,), (0,)), ((), ())), precision=HIGH, preferred_element_type=F32
    ).astype(BF16)


def synth_analyse_body(
    plan, got_ref, point_ref, der_ref, tz_ref, mask_ref, ax_ref, by_ref, gated_ref, slots_ref, acc_ref, s_ref, d_ref
):
    p = plan
    modes = gather_modes(p, got_ref, ax_ref, by_ref, d_ref)
    acc_ref[...] = jnp.zeros_like(acc_ref)

    def group(n, carry):
        first = n * p.step
        weights = forward_weights(p, tz_ref, mask_ref, first)
        synth = lax.dot_general(modes, weights, (((1,), (1,)), ((), ())), preferred_element_type=F32)
        parts = []
        for u in range(p.step):
            middle = (point_ref[first + u] + synth[:, u * p.z : (u + 1) * p.z]).astype(BF16)
            gated = (middle.astype(F32) * der_ref[first + u].astype(F32)).astype(BF16)
            gated_ref[first + u] = gated
            parts.append(gated)
        acc_ref[...] += jnp.dot(jnp.concatenate(parts, axis=1), weights, preferred_element_type=F32)
        return carry

    lax.fori_loop(0, p.c // p.step, group, 0)
    emit_slots(p, acc_ref[...], ax_ref, by_ref, slots_ref, s_ref)


def synth_body(plan, got_ref, point_ref, tz_ref, mask_ref, ax_ref, by_ref, out_ref, d_ref):
    p = plan
    modes = gather_modes(p, got_ref, ax_ref, by_ref, d_ref)

    def group(n, carry):
        first = n * p.step
        weights = forward_weights(p, tz_ref, mask_ref, first)
        synth = lax.dot_general(modes, weights, (((1,), (1,)), ((), ())), preferred_element_type=F32)
        for u in range(p.step):
            out_ref[first + u] = (point_ref[first + u] + synth[:, u * p.z : (u + 1) * p.z]).astype(BF16)
        return carry

    lax.fori_loop(0, p.c // p.step, group, 0)


def pointwise_body(plan, gated_ref, w_ref, spread_ref, out_ref, big_ref):
    p = plan
    n = p.c * p.y
    spread = spread_ref[...]
    rows = lax.dot_general(spread, w_ref[...], (((1,), (1,)), ((), ())), preferred_element_type=F32).astype(BF16)
    both = lax.dot_general(rows, spread, (((1,), (1,)), ((), ())), preferred_element_type=F32)
    same = (
        lax.broadcasted_iota(jnp.int32, (n, n), 0) % p.y == lax.broadcasted_iota(jnp.int32, (n, n), 1) % p.y
    )
    big_ref[...] = jnp.where(same, both, 0.0).astype(BF16)
    for x in range(0, p.x, 2):
        pair = [
            gated_ref[:, (x + h) * p.y : (x + h + 1) * p.y, :].reshape(n, p.z) for h in range(2)
        ]
        out = jnp.dot(big_ref[...], jnp.concatenate(pair, axis=1), preferred_element_type=F32)
        for h in range(2):
            out_ref[:, (x + h) * p.y : (x + h + 1) * p.y, :] = out[:, h * p.z : (h + 1) * p.z].reshape(
                p.c, p.y, p.z
            )


def pack_body(plan, two_ref, one_ref, out_ref):
    p = plan
    out_ref[...] = jnp.zeros_like(out_ref)
    for layer, w_ref in enumerate((two_ref, one_ref)):
        for t in range(p.tiles):
            count = p.valid(t)
            if count == 0:
                continue
            for o in range(p.own):
                for j in range(p.blocks):
                    lanes = [
                        w_ref[
                            pl.ds(((t * p.run) * K + j * p.per_row + q) * p.own + o, count, stride=K * p.own), :
                        ]
                        for q in range(p.per_row)
                    ]
                    out_ref[t, layer, o, j * p.run : j * p.run + count, :] = jnp.concatenate(lanes, axis=1)


def dual_body(plan, got_ref, w_ref, out_ref):
    p = plan
    total = got_ref[0]
    for d in range(1, p.devices):
        total = total + got_ref[d]
    lane = lax.broadcasted_iota(jnp.int32, (SUB, LANES), 1)
    per = p.per_row * p.own
    dual = []
    for r in range(p.slot // SUB):
        part = total[r * SUB : (r + 1) * SUB]
        sums = jnp.zeros((SUB, LANES), F32)
        for o in range(p.c):
            one = jnp.take_along_axis(part, lane // p.c * p.c + o, axis=1)
            sums = sums + one * w_ref[o // p.own, o % p.own, r * SUB : (r + 1) * SUB, :]
        dual.append(sums)
    for t in range(p.tiles):
        piece = jnp.zeros((SUB, LANES), F32)
        for r in range(p.slot // SUB):
            at = lane - r * per
            source = at // p.own * p.c + t * p.own + at % p.own
            source = jnp.clip(source, 0, LANES - 1)
            moved = jnp.take_along_axis(total[r * SUB : (r + 1) * SUB], source, axis=1)
            piece = jnp.where((at >= 0) & (at < per), moved, piece)
        for g in range(p.groups):
            d = g * p.tiles + t
            for r in range(p.slot // SUB):
                out_ref[d, r * SUB : (r + 1) * SUB, :] = dual[r]
            out_ref[d, p.slot :, :] = piece


def grad_body(plan, group_ref, got_ref, saved_ref, out_ref):
    p = plan
    per = p.per_row * p.own
    base = group_ref[0] * p.tiles
    for t in range(p.tiles):
        turned = got_ref[base + t, p.slot :, :].T
        for j in range(p.blocks):
            for r in range(p.valid(t)):
                q = j * p.run + r
                column = turned[q // SUB * per : q // SUB * per + per, q % SUB : q % SUB + 1]
                start = ((t * p.run + r) * K + j * p.per_row) * p.own
                out_ref[start : start + per, :] = saved_ref[start : start + per, :] * column


def solution(mesh):
    def local(cotangent, deriv_two, deriv_one, point_two, point_one, modes_two, modes_one, saved_two, saved_one):
        shape = cotangent.shape
        channels = shape[1]
        plan = p = Plan(mesh, shape[2:], channels)
        xy = p.x * p.y
        g = lax.axis_index("grp")
        t = lax.axis_index("tile")

        full_x, full_y, full_z = basis(p.x * p.groups), basis(p.y * p.tiles), basis(p.z)
        pair = np.full((p.devices, p.run), -1)
        for d in range(p.devices):
            count = p.valid(d % p.tiles)
            pair[d, :count] = d // p.tiles * p.pairs + d % p.tiles * p.run + np.arange(count)
        pair = pair.reshape(-1)
        used = (pair >= 0)[:, None].astype(np.float32)
        rows_x = full_x[np.maximum(pair, 0) // K] * used
        rows_y = full_y[np.maximum(pair, 0) % K]
        rows_x = np.repeat(rows_x.reshape(p.rows, p.groups, p.x).transpose(1, 0, 2), p.y, axis=2)
        rows_y = np.tile(rows_y.reshape(p.rows, p.tiles, p.y).transpose(1, 0, 2), (1, 1, p.x))
        ax = lax.dynamic_index_in_dim(jnp.asarray(rows_x), g, 0, keepdims=False)
        by = lax.dynamic_index_in_dim(jnp.asarray(rows_y), t, 0, keepdims=False)
        tz = jnp.asarray(np.repeat(full_z.T, p.c, axis=1)).astype(BF16)
        mask = np.zeros((p.c, 1, K, p.c), np.float32)
        mask[np.arange(p.c), 0, :, np.arange(p.c)] = 1.0
        mask = jnp.asarray(mask.reshape(p.c, 1, p.width)).astype(BF16)
        spread = jnp.asarray(np.repeat(np.eye(p.c, dtype=np.float32), p.y, axis=0)).astype(BF16)

        field = (p.c, xy, p.z)
        slots = (p.devices, p.slot, LANES)
        packed = (p.devices, p.packed, LANES)
        acc = pltpu.VMEM((xy, p.width), F32)
        s_scr = pltpu.VMEM((p.rows, p.width), F32)

        weights = call(
            pack_body, p, [((p.tiles, 2, p.own, p.slot, LANES), F32)], count=2, name="pack"
        )(modes_two.reshape(-1, channels), modes_one.reshape(-1, channels))[0]
        weights = lax.all_to_all(weights, "tile", 0, 0, tiled=True)

        def exchange(parts):
            return lax.all_to_all(parts, BOTH, 0, 0, tiled=True)

        def dual(got, layer):
            return call(dual_body, p, [(packed, F32)], count=2, name="dual")(got, weights[:, layer])[0]

        def pointwise(gated, w):
            return call(
                pointwise_body, p, [(field, F32)], [pltpu.VMEM((p.c * p.y, p.c * p.y), BF16)], count=3,
                name="pointwise",
            )(gated, w, spread)[0]

        group = jnp.reshape(g, (1,)).astype(jnp.int32)

        def grad(got, saved, like):
            wide = jnp.broadcast_to(saved[0][:, None, :], like.shape).reshape(-1, channels)
            out = call(
                grad_body, p, [(wide.shape, F32)], specs=[SMEM, VMEM, VMEM], name="grad"
            )(group, got, wide)[0]
            return out.reshape(like.shape)

        gated_two, part_two = call(
            analyse_body, p, [(field, BF16), (slots, F32)], [acc, s_scr], count=6, name="analyse"
        )(cotangent.reshape(field), deriv_two.reshape(field), tz, mask, ax, by)
        got_two = exchange(part_two)
        point_out = pointwise(gated_two, point_two)
        all_two = exchange(dual(got_two, 0))
        gated_one, part_one = call(
            synth_analyse_body, p, [(field, BF16), (slots, F32)], [acc, s_scr, s_scr], count=7,
            name="synth_analyse",
        )(all_two, point_out, deriv_one.reshape(field), tz, mask, ax, by)
        got_one = exchange(part_one)
        grad_two = grad(all_two, saved_two, modes_two)
        point_out = pointwise(gated_one, point_one)
        all_one = exchange(dual(got_one, 1))
        result = call(synth_body, p, [(field, BF16)], [s_scr], count=6, name="synth")(
            all_one, point_out, tz, mask, ax, by
        )[0]
        grad_one = grad(all_one, saved_one, modes_one)
        return (result.reshape(shape), grad_one, grad_two)

    return jax.shard_map(
        local,
        mesh=mesh,
        in_specs=(
            P(None, None, "grp", "tile", None),
            P(None, None, "grp", "tile", None),
            P(None, None, "grp", "tile", None),
            P(),
            P(),
            P("grp", "tile", None),
            P("grp", "tile", None),
            P(None, "grp", None),
            P(None, "grp", None),
        ),
        out_specs=(
            P(None, None, "grp", "tile", None),
            P("grp", "tile", None),
            P("grp", "tile", None),
        ),
        check_vma=False,
    )
```

```python
import functools
import math

import jax
import jax.numpy as jnp
import numpy as np
from jax import lax
from jax.experimental import pallas as pl
from jax.experimental.pallas import tpu as pltpu
from jax.sharding import PartitionSpec as P


K = 12
LANES = 128
SUB = 8
COST = 1 << 31
HIGH = lax.Precision.HIGHEST
BOTH = ("grp", "tile")
VMEM = pl.BlockSpec(memory_space=pltpu.VMEM)
HBM = pl.BlockSpec(memory_space=pltpu.HBM)
SMEM = pl.BlockSpec(memory_space=pltpu.SMEM)
F32 = jnp.float32
BF16 = jnp.bfloat16


def basis(length):
    position = np.arange(length)
    orders = np.arange(K)
    frequency = (orders + 1) // 2
    phase = frequency[:, None] * position[None, :] % length
    angle = 2.0 * math.pi / length * phase
    factor = math.sqrt(2.0 / length)
    values = np.where(orders[:, None] % 2 == 1, factor * np.cos(angle), factor * np.sin(angle))
    values[0] = 1.0 / math.sqrt(length)
    return values.astype(np.float32)


class Plan:
    def __init__(self, mesh, cells, channels):
        self.groups, self.tiles = mesh.shape["grp"], mesh.shape["tile"]
        self.devices = self.groups * self.tiles
        self.x, self.y, self.z = cells
        self.c = channels
        self.per_row = LANES // channels
        self.blocks = K // self.per_row
        self.width = K * channels
        self.pairs = K * K // self.groups
        self.run = -(-self.pairs // self.tiles)
        self.slot = -(-self.run * self.blocks // SUB) * SUB
        self.packed = self.slot + SUB
        self.half = self.devices // 2
        self.lanes = self.per_row * self.slot
        self.fold = LANES // self.lanes
        self.rows = self.devices * self.run
        self.own = channels // self.tiles
        self.step = 8

    def valid(self, tile):
        return max(0, min(self.run, self.pairs - self.run * tile))


def call(body, plan, outs, scratch=(), specs=None, out_specs=None, count=None, limit=8, grid=()):
    return pl.pallas_call(
        functools.partial(body, plan),
        grid=grid,
        out_shape=tuple(
            pltpu.HBM(s, d) if spec is not VMEM else jax.ShapeDtypeStruct(s, d)
            for (s, d), spec in zip(outs, out_specs or [VMEM] * len(outs))
        ),
        in_specs=specs or [VMEM] * count,
        out_specs=tuple(out_specs or [VMEM] * len(outs)),
        scratch_shapes=list(scratch),
        compiler_params=pltpu.CompilerParams(vmem_limit_bytes=limit << 20),
        cost_estimate=pl.CostEstimate(flops=COST, bytes_accessed=COST // 1000, transcendentals=0),
    )


def forward_weights(plan, tz_ref, mask_ref, first):
    table = tz_ref[...]
    parts = []
    for u in range(plan.step):
        parts.append(table * mask_ref[first + u])
    return jnp.concatenate(parts, axis=0)


def emit_slots(plan, acc, table, keep_ref, send_ref, s_ref):
    p = plan
    s_ref[...] = jnp.dot(table, acc, precision=HIGH, preferred_element_type=F32)
    for d in range(p.devices):
        slots_ref, n = (keep_ref, d) if d < p.half else (send_ref, d - p.half)
        for j in range(p.blocks):
            slots_ref[n, j * p.run : (j + 1) * p.run, :] = s_ref[
                d * p.run : (d + 1) * p.run, j * LANES : (j + 1) * LANES
            ]
        if p.blocks * p.run < p.slot:
            slots_ref[n, p.blocks * p.run :, :] = jnp.zeros((p.slot - p.blocks * p.run, LANES), F32)


def product(up, der):
    return (up.astype(F32) * der.astype(F32)).astype(BF16)


def spread_rows(rows, cells):
    return lax.dot_general(
        rows, cells, (((0,), (0,)), ((), ())), precision=HIGH, preferred_element_type=F32
    )


def analyse_body(
    plan, place_ref, up_ref, der_hbm, tz_ref, mask_ref, rx_ref, ry_ref, ex_ref, ey_ref,
    keep_ref, send_ref, table_ref, acc_ref, s_ref, der_ref, sems,
):
    p = plan
    step = pl.program_id(0)

    def fetch(n):
        part = pl.ds(n * p.step, p.step)
        return pltpu.make_async_copy(der_hbm.at[part], der_ref.at[part], sems.at[n])

    @pl.when(step == 0)
    def _():
        for n in range(p.c // p.step):
            fetch(n).start()
        table_ref[...] = spread_rows(rx_ref[place_ref[2]], ex_ref[...]) * spread_rows(
            ry_ref[place_ref[3]], ey_ref[...]
        )
        acc_ref[...] = jnp.zeros_like(acc_ref)

    first = step * p.step
    weights = forward_weights(p, tz_ref, mask_ref, first)
    fetch(step).wait()
    parts = []
    for u in range(p.step):
        parts.append(product(up_ref[first + u], der_ref[first + u]))
    acc_ref[...] += jnp.dot(jnp.concatenate(parts, axis=1), weights, preferred_element_type=F32)

    @pl.when(step == pl.num_programs(0) - 1)
    def _():
        emit_slots(p, acc_ref[...], table_ref[...], keep_ref, send_ref, s_ref)


def gather_modes(plan, got_ref, more_ref, table_ref, d_ref):
    p = plan
    for d in range(p.devices):
        from_ref, n = (got_ref, d) if d < p.half else (more_ref, d - p.half)
        for j in range(p.blocks):
            d_ref[d * p.run : (d + 1) * p.run, j * LANES : (j + 1) * LANES] = from_ref[
                n, j * p.run : (j + 1) * p.run, :
            ]
    return lax.dot_general(
        table_ref[...], d_ref[...], (((0,), (0,)), ((), ())), precision=HIGH, preferred_element_type=F32
    ).astype(BF16)


def synth_analyse_body(
    plan, got_ref, more_ref, point_ref, der_ref, tz_ref, mask_ref, table_ref, gated_ref, keep_ref, send_ref,
    acc_ref, s_ref, d_ref, modes_ref, field_ref, sems,
):
    p = plan
    step = pl.program_id(0)

    def store(n):
        part = pl.ds(n * p.step, p.step)
        return pltpu.make_async_copy(field_ref.at[part], gated_ref.at[part], sems.at[n])

    @pl.when(step == 0)
    def _():
        modes_ref[...] = gather_modes(p, got_ref, more_ref, table_ref, d_ref)
        acc_ref[...] = jnp.zeros_like(acc_ref)

    first = step * p.step
    weights = forward_weights(p, tz_ref, mask_ref, first)
    synth = lax.dot_general(modes_ref[...], weights, (((1,), (1,)), ((), ())), preferred_element_type=F32)
    parts = []
    for u in range(p.step):
        middle = (point_ref[first + u] + synth[:, u * p.z : (u + 1) * p.z]).astype(BF16)
        gated = product(middle, der_ref[first + u])
        field_ref[first + u] = gated
        parts.append(gated)
    store(step).start()
    acc_ref[...] += jnp.dot(jnp.concatenate(parts, axis=1), weights, preferred_element_type=F32)

    @pl.when(step == pl.num_programs(0) - 1)
    def _():
        emit_slots(p, acc_ref[...], table_ref[...], keep_ref, send_ref, s_ref)
        for n in range(p.c // p.step):
            store(n).wait()


def synth_body(
    plan, place_ref, got_ref, more_ref, point_ref, tz_ref, mask_ref, table_ref, saved_ref, out_ref, grad_ref,
    d_ref, modes_ref,
):
    p = plan

    @pl.when(pl.program_id(0) == 0)
    def _():
        modes_ref[...] = gather_modes(p, got_ref, more_ref, table_ref, d_ref)
        grad_body(p, place_ref, got_ref, more_ref, saved_ref, grad_ref)

    first = pl.program_id(0) * p.step
    weights = forward_weights(p, tz_ref, mask_ref, first)
    synth = lax.dot_general(modes_ref[...], weights, (((1,), (1,)), ((), ())), preferred_element_type=F32)
    for u in range(p.step):
        out_ref[u] = (point_ref[first + u] + synth[:, u * p.z : (u + 1) * p.z]).astype(BF16)


def pointwise_body(plan, *refs):
    p = plan
    *field_refs, w_ref, spread_ref, out_ref, big_ref = refs
    n = p.c * p.y
    spread = spread_ref[...]
    rows = lax.dot_general(spread, w_ref[...], (((1,), (1,)), ((), ())), preferred_element_type=F32).astype(BF16)
    both = lax.dot_general(rows, spread, (((1,), (1,)), ((), ())), preferred_element_type=F32)
    same = (
        lax.broadcasted_iota(jnp.int32, (n, n), 0) % p.y == lax.broadcasted_iota(jnp.int32, (n, n), 1) % p.y
    )
    big_ref[...] = jnp.where(same, both, 0.0).astype(BF16)
    for x in range(0, p.x, 2):
        pair = []
        for h in range(2):
            cells = [ref[:, (x + h) * p.y : (x + h + 1) * p.y, :] for ref in field_refs]
            pair.append((product(*cells) if len(cells) == 2 else cells[0]).reshape(n, p.z))
        out = jnp.dot(big_ref[...], jnp.concatenate(pair, axis=1), preferred_element_type=F32)
        for h in range(2):
            out_ref[:, (x + h) * p.y : (x + h + 1) * p.y, :] = out[:, h * p.z : (h + 1) * p.z].reshape(
                p.c, p.y, p.z
            )


def pack_body(plan, two_hbm, one_hbm, order_hbm, out_ref, two_ref, one_ref, order_ref, sems):
    p = plan
    n = p.own * p.c
    rows = p.c // p.fold
    copies = [
        pltpu.make_async_copy(source, target, sems.at[n])
        for n, (source, target) in enumerate(((order_hbm, order_ref), (two_hbm, two_ref), (one_hbm, one_ref)))
    ]
    for copy in copies:
        copy.start()
    copies[0].wait()
    for layer, w_ref in enumerate((two_ref, one_ref)):
        copies[1 + layer].wait()
        rest = w_ref[...].reshape(n, p.pairs * K)
        parts = []
        for _ in range(3):
            parts.append(rest.astype(BF16))
            rest = rest - parts[-1].astype(F32)
        moved = jnp.dot(jnp.concatenate(parts, axis=0), order_ref[...], preferred_element_type=F32)
        moved = moved[:n] + moved[n : 2 * n] + moved[2 * n :]
        for o in range(p.own):
            mine = moved[o * p.c : (o + 1) * p.c]
            for t in range(p.tiles):
                out_ref[t, layer, o] = jnp.concatenate(
                    [
                        mine[f * rows : (f + 1) * rows, t * p.lanes : (t + 1) * p.lanes]
                        for f in range(p.fold)
                    ],
                    axis=1,
                )


def dual_body(plan, layer, parity_ref, got_ref, w_ref, out_ref):
    p = plan
    total = got_ref[0]
    for d in range(1, p.half):
        total = total + got_ref[d]
    down = total.T
    ks = [down[k * p.c : (k + 1) * p.c, :] for k in range(p.per_row)]
    modes = jnp.concatenate(ks * p.fold, axis=1)
    rows = p.c // p.fold
    sums = jnp.zeros((rows, LANES), F32)
    for o in range(p.c):
        sums = sums + w_ref[o // p.own, layer, o % p.own] * modes[o : o + 1, :]
    down = sums.T
    pieces = []
    for k in range(p.per_row):
        for f in range(p.fold):
            start = (f * p.per_row + k) * p.slot
            pieces.append(down[start : start + p.slot, :])
    dual = jnp.concatenate(pieces, axis=1)
    parity = parity_ref[0]
    for q in range(p.tiles // 2):
        even = modes[2 * q * p.own : (2 * q + 1) * p.own, :]
        odd = modes[(2 * q + 1) * p.own : (2 * q + 2) * p.own, :]
        mine = jnp.where(parity == 0, even, odd)
        other = jnp.where(parity == 0, odd, even)
        pieces = [mine, other]
        if 2 * p.own < SUB:
            pieces.append(jnp.zeros((SUB - 2 * p.own, LANES), F32))
        both = jnp.concatenate(pieces, axis=0)
        for g in range(p.groups):
            d = g * (p.tiles // 2) + q
            out_ref[d, : p.slot, :] = dual
            out_ref[d, p.slot :, :] = both


def grad_body(plan, place_ref, got_ref, more_ref, saved_ref, out_ref):
    p = plan
    base = place_ref[1] * (p.tiles // 2)
    parity = place_ref[0]
    lane = lax.broadcasted_iota(jnp.int32, (SUB, LANES), 1)
    source = lane % p.per_row * p.slot + lane % K // p.per_row * p.run + lane // K
    source = jnp.clip(source, 0, LANES - 1)
    pieces = []
    for q in range(p.tiles // 2):
        one = jnp.take_along_axis(got_ref[base + q, p.slot :, :], source, axis=1)[: p.own]
        two = jnp.take_along_axis(more_ref[base + q, p.slot :, :], source, axis=1)[p.own : 2 * p.own]
        for t, piece in (
            (2 * q, jnp.where(parity == 0, one, two)),
            (2 * q + 1, jnp.where(parity == 0, two, one)),
        ):
            if p.valid(t) > 0:
                pieces.append(piece[:, : p.valid(t) * K])
    spectrum = jnp.concatenate(pieces, axis=1)
    for o in range(p.own):
        out_ref[o] = saved_ref[...] * spectrum[o : o + 1, :]


def solution(mesh):
    def local(cotangent, deriv_two, deriv_one, point_two, point_one, modes_two, modes_one, saved_two, saved_one):
        shape = cotangent.shape
        channels = shape[1]
        plan = p = Plan(mesh, shape[2:], channels)
        xy = p.x * p.y
        g = lax.axis_index("grp")
        t = lax.axis_index("tile")

        full_x, full_y, full_z = basis(p.x * p.groups), basis(p.y * p.tiles), basis(p.z)
        rows_x, rows_y = [], []
        for parity in range(2):
            pair, used = [], []
            for h in (parity, 1 - parity):
                for d in range(p.half):
                    tile = d % (p.tiles // 2) * 2 + h
                    own = np.arange(p.run)
                    used.append(own < p.valid(tile))
                    start = d // (p.tiles // 2) * p.pairs + tile * p.run
                    pair.append(np.where(used[-1], start + own, 0))
            pair, used = np.concatenate(pair), np.concatenate(used)
            rows_x.append(full_x[pair // K] * used[:, None].astype(np.float32))
            rows_y.append(full_y[pair % K])
        rows_x = np.stack(rows_x).reshape(2, p.rows, p.groups, p.x).transpose(0, 2, 3, 1)
        rows_x = rows_x.reshape(2 * p.groups, p.x, p.rows)
        rows_y = np.stack(rows_y).reshape(2, p.rows, p.tiles // 2, 2, p.y)
        rows_y = np.stack([rows_y[h, :, :, h] for h in range(2)]).transpose(2, 0, 3, 1)
        rows_y = rows_y.reshape(p.tiles, p.y, p.rows)
        parity = t % 2
        rows_x, rows_y = jnp.asarray(rows_x), jnp.asarray(rows_y)
        ex = jnp.asarray(np.repeat(np.eye(p.x, dtype=np.float32), p.y, axis=1))
        ey = jnp.asarray(np.tile(np.eye(p.y, dtype=np.float32), (1, p.x)))
        tz = jnp.asarray(np.repeat(full_z.T, p.c, axis=1)).astype(BF16)
        mask = np.zeros((p.c, 1, K, p.c), np.float32)
        mask[np.arange(p.c), 0, :, np.arange(p.c)] = 1.0
        mask = jnp.asarray(mask.reshape(p.c, 1, p.width)).astype(BF16)
        spread = jnp.asarray(np.repeat(np.eye(p.c, dtype=np.float32), p.y, axis=0)).astype(BF16)

        order = np.zeros((p.pairs * K, p.tiles * p.lanes), np.float32)
        for tile in range(p.tiles):
            for r in range(p.valid(tile)):
                for k in range(K):
                    lane = k % p.per_row * p.slot + k // p.per_row * p.run + r
                    order[(tile * p.run + r) * K + k, tile * p.lanes + lane] = 1.0
        order = jnp.asarray(order).astype(BF16)

        field = (p.c, xy, p.z)
        slots = (p.half, p.slot, LANES)
        packed = (p.half, p.packed, LANES)
        acc = pltpu.VMEM((xy, p.width), F32)
        s_scr = pltpu.VMEM((p.rows, p.width), F32)
        modes_scr = pltpu.VMEM((xy, p.width), BF16)
        blocked = pl.BlockSpec((p.step, xy, p.z), lambda n: (n, 0, 0))
        steps = (p.c // p.step,)
        place = jnp.stack([parity, g, parity * p.groups + g, t]).astype(jnp.int32)
        partners = [(i, i ^ 1) for i in range(p.tiles)]
        same = [
            [e * p.tiles + 2 * q + h for e in range(p.groups) for q in range(p.tiles // 2)] for h in range(2)
        ]

        def in_hbm(array):
            return pltpu.with_memory_space_constraint(array, pltpu.HBM)

        weights = call(
            pack_body, p, [((p.tiles, 2, p.own, p.c // p.fold, LANES), F32)],
            [
                pltpu.VMEM((p.own, p.c, p.pairs * K), F32),
                pltpu.VMEM((p.own, p.c, p.pairs * K), F32),
                pltpu.VMEM(order.shape, BF16),
                pltpu.SemaphoreType.DMA((3,)),
            ],
            specs=[HBM] * 3,
        )(in_hbm(modes_two.transpose(1, 2, 0)), in_hbm(modes_one.transpose(1, 2, 0)), in_hbm(order))[0]
        weights = lax.all_to_all(weights, "tile", 0, 0, tiled=True)

        def exchange(parts):
            return lax.all_to_all(parts, BOTH, 0, 0, tiled=True, axis_index_groups=same)

        def partner(parts):
            return lax.ppermute(parts, "tile", partners)

        def dual(got, layer):
            body = functools.partial(dual_body, p, layer)
            return call(lambda _, *refs: body(*refs), p, [(packed, F32)], specs=[SMEM, VMEM, VMEM])(
                place, got, weights
            )[0]

        def pointwise(w, *factors):
            return call(
                pointwise_body, p, [(field, F32)], [pltpu.VMEM((p.c * p.y, p.c * p.y), BF16)],
                count=2 + len(factors),
            )(*factors, w, spread)[0]

        def grad(got, more, saved):
            out = call(
                grad_body, p, [((p.own, p.c, p.pairs * K), F32)], specs=[SMEM, VMEM, VMEM, VMEM]
            )(place, got, more, saved[0].T)[0]
            return out.transpose(2, 0, 1)

        keep, send, table = call(
            analyse_body, p, [(slots, F32), (slots, F32), ((p.rows, xy), F32)],
            [acc, s_scr, pltpu.VMEM(field, BF16), pltpu.SemaphoreType.DMA(steps)],
            specs=[SMEM, VMEM, HBM] + [VMEM] * 6, grid=steps,
        )(place, cotangent.reshape(field), in_hbm(deriv_two.reshape(field)), tz, mask, rows_x, rows_y, ex, ey)
        part_two = keep + partner(send)
        got_two = exchange(part_two)
        point_out = pointwise(point_two, cotangent.reshape(field), deriv_two.reshape(field))
        share_two = dual(got_two, 0)
        all_two = exchange(share_two)
        more_two = partner(all_two)
        gated_one, keep, send = call(
            synth_analyse_body, p, [(field, BF16), (slots, F32), (slots, F32)], [acc, s_scr, s_scr, modes_scr, pltpu.VMEM(field, BF16), pltpu.SemaphoreType.DMA(steps)],
            count=7, out_specs=[HBM, VMEM, VMEM], grid=steps,
        )(all_two, more_two, point_out, deriv_one.reshape(field), tz, mask, table)
        part_one = keep + partner(send)
        got_one = exchange(part_one)
        grad_two = grad(all_two, more_two, saved_two)
        point_out = pointwise(point_one, gated_one)
        share_one = dual(got_one, 1)
        all_one = exchange(share_one)
        more_one = partner(all_one)
        result, grad_one = call(
            synth_body, p, [(field, BF16), ((p.own, p.c, p.pairs * K), F32)], [s_scr, modes_scr],
            specs=[SMEM] + [VMEM] * 7,
            out_specs=[blocked, pl.BlockSpec((p.own, p.c, p.pairs * K), lambda n: (0, 0, 0))],
            grid=steps,
        )(place, all_one, more_one, point_out, tz, mask, table, saved_one[0].T)
        grad_one = grad_one.transpose(2, 0, 1)
        return (result.reshape(shape), grad_one, grad_two)

    return jax.shard_map(
        local,
        mesh=mesh,
        in_specs=(
            P(None, None, "grp", "tile", None),
            P(None, None, "grp", "tile", None),
            P(None, None, "grp", "tile", None),
            P(),
            P(),
            P("grp", "tile", None),
            P("grp", "tile", None),
            P(None, "grp", None),
            P(None, "grp", None),
        ),
        out_specs=(
            P(None, None, "grp", "tile", None),
            P("grp", "tile", None),
            P("grp", "tile", None),
        ),
        check_vma=False,
    )
```

```python
import functools
import math

import jax
import jax.numpy as jnp
import numpy as np
from jax import lax
from jax.experimental import pallas as pl
from jax.experimental.pallas import tpu as pltpu
from jax.sharding import PartitionSpec as P


K = 12
LANES = 128
SUB = 8
COST = 1 << 31
HIGH = lax.Precision.HIGHEST
BOTH = ("grp", "tile")
VMEM = pl.BlockSpec(memory_space=pltpu.VMEM)
HBM = pl.BlockSpec(memory_space=pltpu.HBM)
SMEM = pl.BlockSpec(memory_space=pltpu.SMEM)
F32 = jnp.float32
BF16 = jnp.bfloat16


def basis(length):
    position = np.arange(length)
    orders = np.arange(K)
    frequency = (orders + 1) // 2
    phase = frequency[:, None] * position[None, :] % length
    angle = 2.0 * math.pi / length * phase
    factor = math.sqrt(2.0 / length)
    values = np.where(orders[:, None] % 2 == 1, factor * np.cos(angle), factor * np.sin(angle))
    values[0] = 1.0 / math.sqrt(length)
    return values.astype(np.float32)


class Plan:
    def __init__(self, mesh, cells, channels):
        self.groups, self.tiles = mesh.shape["grp"], mesh.shape["tile"]
        self.devices = self.groups * self.tiles
        self.x, self.y, self.z = cells
        self.c = channels
        self.per_row = LANES // channels
        self.blocks = K // self.per_row
        self.width = K * channels
        self.pairs = K * K // self.groups
        self.run = -(-self.pairs // self.tiles)
        self.slot = -(-self.run * self.blocks // SUB) * SUB
        self.packed = self.slot + SUB
        self.half = self.devices // 2
        self.chips = self.tiles // 2
        self.lanes = self.per_row * self.slot
        self.fold = LANES // self.lanes
        self.rows = self.devices * self.run
        self.own = channels // self.tiles
        self.step = 8

    def valid(self, tile):
        return max(0, min(self.run, self.pairs - self.run * tile))


def call(body, plan, outs, scratch=(), specs=None, out_specs=None, count=None, limit=8, grid=()):
    return pl.pallas_call(
        functools.partial(body, plan),
        grid=grid,
        out_shape=tuple(
            pltpu.HBM(s, d) if spec is not VMEM else jax.ShapeDtypeStruct(s, d)
            for (s, d), spec in zip(outs, out_specs or [VMEM] * len(outs))
        ),
        in_specs=specs or [VMEM] * count,
        out_specs=tuple(out_specs or [VMEM] * len(outs)),
        scratch_shapes=list(scratch),
        compiler_params=pltpu.CompilerParams(vmem_limit_bytes=limit << 20),
        cost_estimate=pl.CostEstimate(flops=COST, bytes_accessed=COST // 1000, transcendentals=0),
    )


def emit_slots(plan, place_ref, g_ref, order_ref, table_ref, slots_ref, s_ref):
    p = plan
    lines = jnp.concatenate([g_ref[n] for n in range(p.c // p.step)], axis=1)
    lines = lax.dot_general(lines, order_ref[...], (((1,), (1,)), ((), ())), preferred_element_type=F32).astype(BF16)
    both = jnp.dot(table_ref[...], lines, preferred_element_type=F32)
    s_ref[...] = both[: p.rows] + both[p.rows :]
    for d in range(p.devices):
        parity = place_ref[0] if d < p.half else 1 - place_ref[0]
        n = (d % p.half // p.chips) * p.tiles + d % p.chips * 2 + parity
        for j in range(p.blocks):
            slots_ref[n, j * p.run : (j + 1) * p.run, :] = s_ref[
                d * p.run : (d + 1) * p.run, j * LANES : (j + 1) * LANES
            ]
        if p.blocks * p.run < p.slot:
            slots_ref[n, p.blocks * p.run :, :] = jnp.zeros((p.slot - p.blocks * p.run, LANES), F32)


def product(up, der):
    return (up.astype(F32) * der.astype(F32)).astype(BF16)


def spread_rows(rows, cells):
    return lax.dot_general(
        rows, cells, (((0,), (0,)), ((), ())), precision=HIGH, preferred_element_type=F32
    )


def analyse_body(
    plan, place_ref, up_ref, der_hbm, tz_ref, order_ref, rx_ref, ry_ref, ex_ref, ey_ref,
    slots_ref, table_hbm, turned_hbm, g_ref, s_ref, der_ref, table_ref, turned_ref, sems,
):
    p = plan
    step = pl.program_id(0)

    def fetch(n):
        part = pl.ds(n * p.step, p.step)
        return pltpu.make_async_copy(der_hbm.at[part], der_ref.at[part], sems.at[n])

    last = p.c // p.step
    tables = (
        pltpu.make_async_copy(table_ref, table_hbm, sems.at[last]),
        pltpu.make_async_copy(turned_ref, turned_hbm, sems.at[last + 1]),
    )

    @pl.when(step == 0)
    def _():
        for n in range(p.c // p.step):
            fetch(n).start()
        table = spread_rows(rx_ref[place_ref[2]], ex_ref[...]) * spread_rows(ry_ref[place_ref[3]], ey_ref[...])
        high = table.astype(BF16)
        table_ref[: p.rows] = high
        table_ref[p.rows :] = (table - high.astype(F32)).astype(BF16)
        turned_ref[...] = table.T.astype(BF16)
        for copy in tables:
            copy.start()

    first = step * p.step
    fetch(step).wait()
    parts = [product(up_ref[first + u], der_ref[first + u]) for u in range(p.step)]
    g_ref[step] = lax.dot_general(
        jnp.concatenate(parts, axis=1), tz_ref[...], (((1,), (1,)), ((), ())), preferred_element_type=F32
    ).astype(BF16)

    @pl.when(step == pl.num_programs(0) - 1)
    def _():
        emit_slots(p, place_ref, g_ref, order_ref, table_ref, slots_ref, s_ref)
        for copy in tables:
            copy.wait()


def gather_modes(plan, got_ref, more_ref, order_ref, turned_ref, d_ref, modes_ref, ready=None):
    p = plan
    for d in range(p.devices):
        from_ref, n = (got_ref, d) if d < p.half else (more_ref, d - p.half)
        for j in range(p.blocks):
            d_ref[d * p.run : (d + 1) * p.run, j * LANES : (j + 1) * LANES] = from_ref[
                n, j * p.run : (j + 1) * p.run, :
            ]
    if ready is not None:
        ready()
    lines = jnp.dot(turned_ref[...], d_ref[...].astype(BF16), preferred_element_type=F32).astype(BF16)
    lines = jnp.dot(lines, order_ref[...], preferred_element_type=F32).astype(BF16)
    for n in range(p.c // p.step):
        modes_ref[n] = lines[:, n * LANES : (n + 1) * LANES]


def synth_analyse_body(
    plan, place_ref, got_ref, more_ref, point_ref, der_ref, order_ref, tz_hbm, turned_hbm, table_hbm,
    gated_ref, slots_ref, g_ref, s_ref, d_ref, modes_ref, field_ref, tz_ref, turned_ref, table_ref, sems, table_sems,
):
    p = plan
    step = pl.program_id(0)
    pairs = ((turned_hbm, turned_ref), (tz_hbm, tz_ref), (table_hbm, table_ref))
    tables = [pltpu.make_async_copy(*pair, table_sems.at[n]) for n, pair in enumerate(pairs)]

    def store(n):
        part = pl.ds(n * p.step, p.step)
        return pltpu.make_async_copy(field_ref.at[part], gated_ref.at[part], sems.at[n])

    @pl.when(step == 0)
    def _():
        for copy in tables:
            copy.start()
        gather_modes(p, got_ref, more_ref, order_ref, turned_ref, d_ref, modes_ref, tables[0].wait)
        for copy in tables[1:]:
            copy.wait()

    first = step * p.step
    synth = jnp.dot(modes_ref[step], tz_ref[...], preferred_element_type=F32)
    parts = []
    for u in range(p.step):
        middle = (point_ref[first + u] + synth[:, u * p.z : (u + 1) * p.z]).astype(BF16)
        gated = product(middle, der_ref[first + u])
        field_ref[first + u] = gated
        parts.append(gated)
    store(step).start()
    g_ref[step] = lax.dot_general(
        jnp.concatenate(parts, axis=1), tz_ref[...], (((1,), (1,)), ((), ())), preferred_element_type=F32
    ).astype(BF16)

    @pl.when(step == pl.num_programs(0) - 1)
    def _():
        emit_slots(p, place_ref, g_ref, order_ref, table_ref, slots_ref, s_ref)
        for n in range(p.c // p.step):
            store(n).wait()


def synth_body(
    plan, place_ref, got_ref, more_ref, point_ref, tz_ref, order_ref, turned_ref, saved_ref, out_ref, grad_ref,
    d_ref, modes_ref,
):
    p = plan
    step = pl.program_id(0)

    @pl.when(step == 0)
    def _():
        gather_modes(p, got_ref, more_ref, order_ref, turned_ref, d_ref, modes_ref)
        grad_body(p, place_ref, got_ref, more_ref, saved_ref, grad_ref)

    first = step * p.step
    synth = jnp.dot(modes_ref[step], tz_ref[...], preferred_element_type=F32)
    for u in range(p.step):
        out_ref[u] = (point_ref[first + u] + synth[:, u * p.z : (u + 1) * p.z]).astype(BF16)


def pointwise_body(plan, *refs):
    p = plan
    *field_refs, w_ref, spread_ref, out_ref, big_ref = refs
    n = p.c * p.y
    spread = spread_ref[...]
    rows = lax.dot_general(spread, w_ref[...], (((1,), (1,)), ((), ())), preferred_element_type=F32).astype(BF16)
    both = lax.dot_general(rows, spread, (((1,), (1,)), ((), ())), preferred_element_type=F32)
    same = (
        lax.broadcasted_iota(jnp.int32, (n, n), 0) % p.y == lax.broadcasted_iota(jnp.int32, (n, n), 1) % p.y
    )
    big_ref[...] = jnp.where(same, both, 0.0).astype(BF16)
    for x in range(0, p.x, 2):
        pair = []
        for h in range(2):
            cells = [ref[:, (x + h) * p.y : (x + h + 1) * p.y, :] for ref in field_refs]
            pair.append((product(*cells) if len(cells) == 2 else cells[0]).reshape(n, p.z))
        out = jnp.dot(big_ref[...], jnp.concatenate(pair, axis=1), preferred_element_type=F32)
        for h in range(2):
            out_ref[:, (x + h) * p.y : (x + h + 1) * p.y, :] = out[:, h * p.z : (h + 1) * p.z].reshape(
                p.c, p.y, p.z
            )


def pack_body(plan, place_ref, two_hbm, one_hbm, order_hbm, *refs):
    p = plan
    *out_refs, two_ref, one_ref, order_ref, sems = refs
    n = p.own * p.c
    rows = p.c // p.fold
    copies = [
        pltpu.make_async_copy(two_hbm, two_ref, sems.at[0]),
        pltpu.make_async_copy(order_hbm.at[place_ref[3] // 2], order_ref, sems.at[1]),
        pltpu.make_async_copy(one_hbm, one_ref, sems.at[2]),
    ]
    for copy in copies:
        copy.start()
    for layer, w_ref in enumerate((two_ref, one_ref)):
        copies[2 * layer].wait()
        rest = w_ref[...].reshape(n, p.pairs * K)
        parts = []
        for _ in range(2):
            parts.append(rest.astype(BF16))
            rest = rest - parts[-1].astype(F32)
        if layer == 0:
            copies[1].wait()
        moved = jnp.dot(jnp.concatenate(parts, axis=0), order_ref[...], preferred_element_type=F32)
        moved = moved[:n] + moved[n:]
        for o in range(p.own):
            mine = moved[o * p.c : (o + 1) * p.c]
            for t in range(p.tiles):
                core = jnp.bitwise_xor(place_ref[0], t % 2)
                out_refs[t // 2][core, layer, o] = jnp.concatenate(
                    [mine[f * rows : (f + 1) * rows, t * p.lanes : (t + 1) * p.lanes] for f in range(p.fold)], axis=1
                )


def dual_body(plan, layer, place_ref, got_ref, *refs):
    p = plan
    *w_refs, cross_ref, out_ref, modes_ref = refs
    total = got_ref[0]
    for d in range(1, p.devices):
        total = total + got_ref[d]
    down = total.T
    ks = [down[k * p.c : (k + 1) * p.c, :] for k in range(p.per_row)]
    modes = jnp.concatenate(ks * p.fold, axis=1)
    modes_ref[...] = modes
    rows = p.c // p.fold
    sums = jnp.zeros((rows, LANES), F32)
    for chip in range(p.chips):
        for core in range(2):
            tile = jnp.bitwise_xor(place_ref[3] // 2, chip) * 2 + jnp.bitwise_xor(place_ref[0], core)
            for o in range(p.own):
                w = cross_ref[chip, layer, o] if core else w_refs[chip][0, layer, o]
                sums = sums + w * modes_ref[pl.ds(tile * p.own + o, 1), :]
    down = sums.T
    pieces = []
    for k in range(p.per_row):
        for f in range(p.fold):
            start = (f * p.per_row + k) * p.slot
            pieces.append(down[start : start + p.slot, :])
    dual = jnp.concatenate(pieces, axis=1)
    parity = place_ref[0]
    for q in range(p.tiles // 2):
        even = modes[2 * q * p.own : (2 * q + 1) * p.own, :]
        odd = modes[(2 * q + 1) * p.own : (2 * q + 2) * p.own, :]
        mine = jnp.where(parity == 0, even, odd)
        other = jnp.where(parity == 0, odd, even)
        pieces = [mine, other]
        if 2 * p.own < SUB:
            pieces.append(jnp.zeros((SUB - 2 * p.own, LANES), F32))
        both = jnp.concatenate(pieces, axis=0)
        for g in range(p.groups):
            d = g * (p.tiles // 2) + q
            out_ref[d, : p.slot, :] = dual
            out_ref[d, p.slot :, :] = both


def grad_body(plan, place_ref, got_ref, more_ref, saved_ref, out_ref):
    p = plan
    base = place_ref[1] * (p.tiles // 2)
    parity = place_ref[0]
    lane = lax.broadcasted_iota(jnp.int32, (SUB, LANES), 1)
    source = lane % p.per_row * p.slot + lane % K // p.per_row * p.run + lane // K
    source = jnp.clip(source, 0, LANES - 1)
    pieces = []
    for q in range(p.tiles // 2):
        one = jnp.take_along_axis(got_ref[base + q, p.slot :, :], source, axis=1)[: p.own]
        two = jnp.take_along_axis(more_ref[base + q, p.slot :, :], source, axis=1)[p.own : 2 * p.own]
        for t, piece in (
            (2 * q, jnp.where(parity == 0, one, two)),
            (2 * q + 1, jnp.where(parity == 0, two, one)),
        ):
            if p.valid(t) > 0:
                pieces.append(piece[:, : p.valid(t) * K])
    spectrum = jnp.concatenate(pieces, axis=1)
    for o in range(p.own):
        out_ref[o] = saved_ref[...] * spectrum[o : o + 1, :]


def solution(mesh):
    def local(cotangent, deriv_two, deriv_one, point_two, point_one, modes_two, modes_one, saved_two, saved_one):
        shape = cotangent.shape
        channels = shape[1]
        plan = p = Plan(mesh, shape[2:], channels)
        xy = p.x * p.y
        g = lax.axis_index("grp")
        t = lax.axis_index("tile")

        full_x, full_y, full_z = basis(p.x * p.groups), basis(p.y * p.tiles), basis(p.z)
        rows_x, rows_y = [], []
        for parity in range(2):
            pair, used = [], []
            for h in (parity, 1 - parity):
                for d in range(p.half):
                    tile = d % (p.tiles // 2) * 2 + h
                    own = np.arange(p.run)
                    used.append(own < p.valid(tile))
                    start = d // (p.tiles // 2) * p.pairs + tile * p.run
                    pair.append(np.where(used[-1], start + own, 0))
            pair, used = np.concatenate(pair), np.concatenate(used)
            rows_x.append(full_x[pair // K] * used[:, None].astype(np.float32))
            rows_y.append(full_y[pair % K])
        rows_x = np.stack(rows_x).reshape(2, p.rows, p.groups, p.x).transpose(0, 2, 3, 1)
        rows_x = rows_x.reshape(2 * p.groups, p.x, p.rows)
        rows_y = np.stack(rows_y).reshape(2, p.rows, p.tiles // 2, 2, p.y)
        rows_y = np.stack([rows_y[h, :, :, h] for h in range(2)]).transpose(2, 0, 3, 1)
        rows_y = rows_y.reshape(p.tiles, p.y, p.rows)
        parity = t % 2
        rows_x, rows_y = jnp.asarray(rows_x), jnp.asarray(rows_y)
        ex = jnp.asarray(np.repeat(np.eye(p.x, dtype=np.float32), p.y, axis=1))
        ey = jnp.asarray(np.tile(np.eye(p.y, dtype=np.float32), (1, p.x)))
        groups = p.c // p.step
        tz = np.zeros((LANES, p.step, p.z), np.float32)
        lines = np.zeros((K, groups, p.step, groups, LANES), np.float32)
        for u in range(p.step):
            for k in range(K):
                tz[k * p.step + u, u] = full_z[k]
                lines[k, np.arange(groups), u, np.arange(groups), k * p.step + u] = 1.0
        tz = jnp.asarray(tz.reshape(LANES, p.step * p.z)).astype(BF16)
        lines = jnp.asarray(lines.reshape(p.width, groups * LANES)).astype(BF16)
        spread = jnp.asarray(np.repeat(np.eye(p.c, dtype=np.float32), p.y, axis=0)).astype(BF16)

        order = np.zeros((p.chips, p.pairs * K, p.tiles * p.lanes), np.float32)
        for chip in range(p.chips):
            for tile in range(p.tiles):
                at = ((tile // 2 ^ chip) * 2 + tile % 2) * p.lanes
                for r in range(p.valid(tile)):
                    for k in range(K):
                        lane = k % p.per_row * p.slot + k // p.per_row * p.run + r
                        order[chip, (tile * p.run + r) * K + k, at + lane] = 1.0
        order = jnp.asarray(order).astype(BF16)

        field = (p.c, xy, p.z)
        slots = (p.devices, p.slot, LANES)
        packed = (p.half, p.packed, LANES)
        g_scr = pltpu.VMEM((groups, xy, LANES), BF16)
        s_scr = pltpu.VMEM((p.rows, p.width), F32)
        modes_scr = g_scr
        blocked = pl.BlockSpec((p.step, xy, p.z), lambda n: (n, 0, 0))
        steps = (p.c // p.step,)
        place = jnp.stack([parity, g, parity * p.groups + g, t]).astype(jnp.int32)
        partners = [(i, i ^ 1) for i in range(p.tiles)]
        same = [
            [e * p.tiles + 2 * q + h for e in range(p.groups) for q in range(p.tiles // 2)] for h in range(2)
        ]

        def in_hbm(array):
            return pltpu.with_memory_space_constraint(array, pltpu.HBM)

        packs = call(
            pack_body, p, [((2, 2, p.own, p.c // p.fold, LANES), F32)] * p.chips,
            [
                pltpu.VMEM((p.own, p.c, p.pairs * K), F32),
                pltpu.VMEM((p.own, p.c, p.pairs * K), F32),
                pltpu.VMEM(order.shape[1:], BF16),
                pltpu.SemaphoreType.DMA((3,)),
            ],
            specs=[SMEM] + [HBM] * 3,
        )(place, in_hbm(modes_two.transpose(1, 2, 0)), in_hbm(modes_one.transpose(1, 2, 0)), in_hbm(order))
        dealt = [packs[0]]
        for chip in range(1, p.chips):
            dealt.append(lax.ppermute(packs[chip], "tile", [(i, i ^ (2 * chip)) for i in range(p.tiles)]))
        crossing = jnp.stack([part[1] for part in dealt])
        crossed = lax.ppermute(crossing, "tile", partners)

        def exchange(parts):
            return lax.all_to_all(parts, BOTH, 0, 0, tiled=True, axis_index_groups=same)

        def partner(parts):
            return lax.ppermute(parts, "tile", partners)

        def dual(got, layer):
            body = functools.partial(dual_body, p, layer)
            return call(
                lambda _, *refs: body(*refs), p, [(packed, F32)], [pltpu.VMEM((p.c, LANES), F32)],
                specs=[SMEM] + [VMEM] * (p.chips + 2),
            )(place, got, *dealt, crossed)[0]

        def pointwise(w, *factors):
            return call(
                pointwise_body, p, [(field, F32)], [pltpu.VMEM((p.c * p.y, p.c * p.y), BF16)],
                count=2 + len(factors),
            )(*factors, w, spread)[0]

        def grad(got, more, saved):
            out = call(
                grad_body, p, [((p.own, p.c, p.pairs * K), F32)], specs=[SMEM, VMEM, VMEM, VMEM]
            )(place, got, more, saved[0].T)[0]
            return out.transpose(2, 0, 1)

        part_two, table, turned = call(
            analyse_body, p, [(slots, F32), ((2 * p.rows, xy), BF16), ((xy, p.rows), BF16)],
            [
                g_scr, s_scr, pltpu.VMEM(field, BF16), pltpu.VMEM((2 * p.rows, xy), BF16),
                pltpu.VMEM((xy, p.rows), BF16), pltpu.SemaphoreType.DMA((groups + 2,)),
            ],
            specs=[SMEM, VMEM, HBM] + [VMEM] * 6, out_specs=[VMEM, HBM, HBM], grid=steps,
        )(place, cotangent.reshape(field), in_hbm(deriv_two.reshape(field)), tz, lines, rows_x, rows_y, ex, ey)
        got_two = lax.all_to_all(part_two, BOTH, 0, 0, tiled=True)
        point_out = pointwise(point_two, cotangent.reshape(field), deriv_two.reshape(field))
        share_two = dual(got_two, 0)
        all_two = exchange(share_two)
        more_two = partner(all_two)
        gated_one, part_one = call(
            synth_analyse_body, p, [(field, BF16), (slots, F32)], [
                g_scr, s_scr, s_scr, modes_scr, pltpu.VMEM(field, BF16), pltpu.VMEM(tz.shape, BF16),
                pltpu.VMEM(turned.shape, BF16), pltpu.VMEM(table.shape, BF16),
                pltpu.SemaphoreType.DMA(steps), pltpu.SemaphoreType.DMA((3,)),
            ],
            specs=[SMEM] + [VMEM] * 5 + [HBM] * 3, out_specs=[HBM, VMEM], grid=steps,
        )(place, all_two, more_two, point_out, deriv_one.reshape(field), lines, in_hbm(tz), in_hbm(turned), in_hbm(table))
        got_one = lax.all_to_all(part_one, BOTH, 0, 0, tiled=True)
        grad_two = grad(all_two, more_two, saved_two)
        point_out = pointwise(point_one, gated_one)
        share_one = dual(got_one, 1)
        all_one = exchange(share_one)
        more_one = partner(all_one)
        result, grad_one = call(
            synth_body, p, [(field, BF16), ((p.own, p.c, p.pairs * K), F32)], [s_scr, modes_scr],
            specs=[SMEM] + [VMEM] * 7,
            out_specs=[blocked, pl.BlockSpec((p.own, p.c, p.pairs * K), lambda n: (0, 0, 0))],
            grid=steps,
        )(place, all_one, more_one, point_out, tz, lines, turned, saved_one[0].T)
        grad_one = grad_one.transpose(2, 0, 1)
        return (result.reshape(shape), grad_one, grad_two)

    return jax.shard_map(
        local,
        mesh=mesh,
        in_specs=(
            P(None, None, "grp", "tile", None),
            P(None, None, "grp", "tile", None),
            P(None, None, "grp", "tile", None),
            P(),
            P(),
            P("grp", "tile", None),
            P("grp", "tile", None),
            P(None, "grp", None),
            P(None, "grp", None),
        ),
        out_specs=(
            P(None, None, "grp", "tile", None),
            P("grp", "tile", None),
            P("grp", "tile", None),
        ),
        check_vma=False,
    )
```

```python
import functools
import math

import jax
import jax.numpy as jnp
import numpy as np
from jax import lax
from jax.experimental import pallas as pl
from jax.experimental.pallas import tpu as pltpu
from jax.sharding import PartitionSpec as P


K = 12
LANES = 128
SUB = 8
COST = 1 << 31
BOTH = ("grp", "tile")
VMEM = pl.BlockSpec(memory_space=pltpu.VMEM)
HBM = pl.BlockSpec(memory_space=pltpu.HBM)
F32 = jnp.float32
BF16 = jnp.bfloat16


def basis(length):
    position = np.arange(length)
    orders = np.arange(K)
    frequency = (orders + 1) // 2
    phase = frequency[:, None] * position[None, :] % length
    angle = 2.0 * math.pi / length * phase
    factor = math.sqrt(2.0 / length)
    values = np.where(orders[:, None] % 2 == 1, factor * np.cos(angle), factor * np.sin(angle))
    values[0] = 1.0 / math.sqrt(length)
    return values.astype(np.float32)


def place_of(plan):
    group, tile = lax.axis_index("grp"), lax.axis_index("tile")
    parity = jnp.bitwise_and(tile, 1)
    return parity, group, parity * plan.groups + group, tile


def two_parts(table):
    high = table.astype(jnp.bfloat16)
    return jnp.asarray(np.concatenate([high, (table - high.astype(np.float32)).astype(jnp.bfloat16)], axis=1))


class Plan:
    def __init__(self, mesh, cells, channels):
        self.groups, self.tiles = mesh.shape["grp"], mesh.shape["tile"]
        self.devices = self.groups * self.tiles
        self.x, self.y, self.z = cells
        self.c = channels
        self.per_row = LANES // channels
        self.blocks = K // self.per_row
        self.width = K * channels
        self.pairs = K * K // self.groups
        self.run = -(-self.pairs // self.tiles)
        self.slot = -(-self.run * self.blocks // SUB) * SUB
        self.packed = self.slot + SUB
        self.half = self.devices // 2
        self.chips = self.tiles // 2
        self.lanes = self.per_row * self.slot
        self.fold = LANES // self.lanes
        self.rows = self.devices * self.run
        self.own = channels // self.tiles
        self.step = 8

    def valid(self, tile):
        return max(0, min(self.run, self.pairs - self.run * tile))


def call(body, plan, outs, scratch=(), specs=None, out_specs=None, count=None, limit=8, grid=()):
    return pl.pallas_call(
        functools.partial(body, plan),
        grid=grid,
        out_shape=tuple(
            pltpu.HBM(s, d) if spec is not VMEM else jax.ShapeDtypeStruct(s, d)
            for (s, d), spec in zip(outs, out_specs or [VMEM] * len(outs))
        ),
        in_specs=specs or [VMEM] * count,
        out_specs=tuple(out_specs or [VMEM] * len(outs)),
        scratch_shapes=list(scratch),
        compiler_params=pltpu.CompilerParams(vmem_limit_bytes=limit << 20),
        cost_estimate=pl.CostEstimate(flops=COST, bytes_accessed=COST // 1000, transcendentals=0),
    )


def emit_slots(plan, g_ref, order_ref, table_ref, slots_ref, s_ref):
    p = plan
    place_ref = place_of(p)
    lines = jnp.concatenate([g_ref[n] for n in range(p.c // p.step)], axis=1)
    lines = lax.dot_general(lines, order_ref[...], (((1,), (1,)), ((), ())), preferred_element_type=F32).astype(BF16)
    both = jnp.dot(table_ref[...], lines, preferred_element_type=F32)
    s_ref[...] = both[: p.rows] + both[p.rows :]
    for d in range(p.devices):
        parity = place_ref[0] if d < p.half else 1 - place_ref[0]
        n = (d % p.half // p.chips) * p.tiles + d % p.chips * 2 + parity
        for j in range(p.blocks):
            slots_ref[n, j * p.run : (j + 1) * p.run, :] = s_ref[
                d * p.run : (d + 1) * p.run, j * LANES : (j + 1) * LANES
            ]
        if p.blocks * p.run < p.slot:
            slots_ref[n, p.blocks * p.run :, :] = jnp.zeros((p.slot - p.blocks * p.run, LANES), F32)


def product(up, der):
    return (up.astype(F32) * der.astype(F32)).astype(BF16)


def spread_rows(rows, cells):
    return lax.dot_general(rows, cells, (((0,), (0,)), ((), ())), preferred_element_type=F32)


def analyse_body(
    plan, up_ref, der_hbm, tz_ref, order_ref, rx_ref, ry_ref, ex_ref, ey_ref,
    slots_ref, table_hbm, turned_hbm, g_ref, s_ref, der_ref, table_ref, turned_ref, sems,
):
    p = plan
    place_ref = place_of(p)
    step = pl.program_id(0)

    def fetch(n):
        part = pl.ds(n * p.step, p.step)
        return pltpu.make_async_copy(der_hbm.at[part], der_ref.at[part], sems.at[n])

    last = p.c // p.step
    tables = (
        pltpu.make_async_copy(table_ref, table_hbm, sems.at[last]),
        pltpu.make_async_copy(turned_ref, turned_hbm, sems.at[last + 1]),
    )

    @pl.when(step == 0)
    def _():
        for n in range(p.c // p.step):
            fetch(n).start()
        table = spread_rows(rx_ref[place_ref[2]], ex_ref[...]) * spread_rows(ry_ref[place_ref[3]], ey_ref[...])
        high = table.astype(BF16)
        table_ref[: p.rows] = high
        table_ref[p.rows :] = (table - high.astype(F32)).astype(BF16)
        turned_ref[...] = table.T.astype(BF16)
        for copy in tables:
            copy.start()

    first = step * p.step
    fetch(step).wait()
    parts = [product(up_ref[first + u], der_ref[first + u]) for u in range(p.step)]
    g_ref[step] = lax.dot_general(
        jnp.concatenate(parts, axis=1), tz_ref[...], (((1,), (1,)), ((), ())), preferred_element_type=F32
    ).astype(BF16)

    @pl.when(step == pl.num_programs(0) - 1)
    def _():
        emit_slots(p, g_ref, order_ref, table_ref, slots_ref, s_ref)
        for copy in tables:
            copy.wait()


def gather_modes(plan, got_ref, more_ref, order_ref, turned_ref, d_ref, modes_ref, ready=None):
    p = plan
    for d in range(p.devices):
        from_ref, n = (got_ref, d) if d < p.half else (more_ref, d - p.half)
        for j in range(p.blocks):
            d_ref[d * p.run : (d + 1) * p.run, j * LANES : (j + 1) * LANES] = from_ref[
                n, j * p.run : (j + 1) * p.run, :
            ]
    if ready is not None:
        ready()
    lines = jnp.dot(turned_ref[...], d_ref[...].astype(BF16), preferred_element_type=F32).astype(BF16)
    lines = jnp.dot(lines, order_ref[...], preferred_element_type=F32).astype(BF16)
    for n in range(p.c // p.step):
        modes_ref[n] = lines[:, n * LANES : (n + 1) * LANES]


def synth_analyse_body(
    plan, got_ref, more_ref, point_ref, der_ref, order_ref, tz_hbm, turned_hbm, table_hbm,
    gated_ref, slots_ref, g_ref, s_ref, d_ref, modes_ref, field_ref, tz_ref, turned_ref, table_ref, sems, table_sems,
):
    p = plan
    step = pl.program_id(0)
    pairs = ((turned_hbm, turned_ref), (tz_hbm, tz_ref), (table_hbm, table_ref))
    tables = [pltpu.make_async_copy(*pair, table_sems.at[n]) for n, pair in enumerate(pairs)]

    def store(n):
        part = pl.ds(n * p.step, p.step)
        return pltpu.make_async_copy(field_ref.at[part], gated_ref.at[part], sems.at[n])

    @pl.when(step == 0)
    def _():
        for copy in tables:
            copy.start()
        gather_modes(p, got_ref, more_ref, order_ref, turned_ref, d_ref, modes_ref, tables[0].wait)
        for copy in tables[1:]:
            copy.wait()

    first = step * p.step
    synth = jnp.dot(modes_ref[step], tz_ref[...], preferred_element_type=F32)
    parts = []
    for u in range(p.step):
        middle = (point_ref[first + u] + synth[:, u * p.z : (u + 1) * p.z]).astype(BF16)
        gated = product(middle, der_ref[first + u])
        field_ref[first + u] = gated
        parts.append(gated)
    store(step).start()
    g_ref[step] = lax.dot_general(
        jnp.concatenate(parts, axis=1), tz_ref[...], (((1,), (1,)), ((), ())), preferred_element_type=F32
    ).astype(BF16)

    @pl.when(step == pl.num_programs(0) - 1)
    def _():
        emit_slots(p, g_ref, order_ref, table_ref, slots_ref, s_ref)
        for n in range(p.c // p.step):
            store(n).wait()


def synth_body(
    plan, got_ref, more_ref, point_ref, tz_ref, order_ref, turned_ref, saved_ref, out_ref, grad_ref,
    d_ref, modes_ref,
):
    p = plan
    step = pl.program_id(0)

    @pl.when(step == 0)
    def _():
        gather_modes(p, got_ref, more_ref, order_ref, turned_ref, d_ref, modes_ref)
        grad_body(p, got_ref, more_ref, saved_ref, grad_ref)

    first = step * p.step
    synth = jnp.dot(modes_ref[step], tz_ref[...], preferred_element_type=F32)
    for u in range(p.step):
        out_ref[u] = (point_ref[first + u] + synth[:, u * p.z : (u + 1) * p.z]).astype(BF16)


def pointwise_body(plan, *refs):
    p = plan
    *field_refs, w_ref, spread_ref, out_ref, big_ref = refs
    n = p.c * p.y
    spread = spread_ref[...]
    rows = lax.dot_general(spread, w_ref[...], (((1,), (1,)), ((), ())), preferred_element_type=F32).astype(BF16)
    both = lax.dot_general(rows, spread, (((1,), (1,)), ((), ())), preferred_element_type=F32)
    same = (
        lax.broadcasted_iota(jnp.int32, (n, n), 0) % p.y == lax.broadcasted_iota(jnp.int32, (n, n), 1) % p.y
    )
    big_ref[...] = jnp.where(same, both, 0.0).astype(BF16)
    for x in range(0, p.x, 2):
        pair = []
        for h in range(2):
            cells = [ref[:, (x + h) * p.y : (x + h + 1) * p.y, :] for ref in field_refs]
            pair.append((product(*cells) if len(cells) == 2 else cells[0]).reshape(n, p.z))
        out = jnp.dot(big_ref[...], jnp.concatenate(pair, axis=1), preferred_element_type=F32)
        for h in range(2):
            out_ref[:, (x + h) * p.y : (x + h + 1) * p.y, :] = out[:, h * p.z : (h + 1) * p.z].reshape(
                p.c, p.y, p.z
            )


def pack_body(plan, two_hbm, one_hbm, target_hbm, odd_ref, *refs):
    p = plan
    place_ref = place_of(p)
    *even_refs, two_ref, one_ref, target_ref, order_ref, sems = refs
    n = p.own * p.c
    rows = p.c // p.fold
    copies = [
        pltpu.make_async_copy(two_hbm, two_ref, sems.at[0]),
        pltpu.make_async_copy(one_hbm, one_ref, sems.at[1]),
        pltpu.make_async_copy(target_hbm, target_ref, sems.at[2]),
    ]
    for copy in (copies[2], *copies[:2]):
        copy.start()
    copies[2].wait()
    mode = lax.broadcasted_iota(jnp.int32, order_ref.shape, 0)
    order_ref[...] = jnp.where(mode == target_ref[lax.div(place_ref[3], 2)], 1.0, 0.0).astype(BF16)
    for layer, w_ref in enumerate((two_ref, one_ref)):
        copies[layer].wait()
        rest = w_ref[...].reshape(n, p.pairs * K)
        parts = []
        for _ in range(2):
            parts.append(rest.astype(BF16))
            rest = rest - parts[-1].astype(F32)
        moved = jnp.dot(jnp.concatenate(parts, axis=0), order_ref[...], preferred_element_type=F32)
        moved = moved[:n] + moved[n:]
        for o in range(p.own):
            mine = moved[o * p.c : (o + 1) * p.c]
            for t in range(p.tiles):
                core = jnp.bitwise_xor(place_ref[0], t % 2)
                chip = t // 2
                block = jnp.concatenate(
                    [mine[f * rows : (f + 1) * rows, t * p.lanes : (t + 1) * p.lanes] for f in range(p.fold)], axis=1
                )
                if chip % 2:
                    odd_ref[chip // 2, core, layer, o] = block
                else:
                    even_refs[chip // 2][core, layer, o] = block


def dual_body(plan, got_ref, *refs):
    p = plan
    place_ref = place_of(p)
    w_refs, cross_ref, out_ref, modes_ref = refs[: p.chips], *refs[p.chips :]
    total = got_ref[0]
    for d in range(1, p.devices):
        total = total + got_ref[d]
    down = total.T
    ks = [down[k * p.c : (k + 1) * p.c, :] for k in range(p.per_row)]
    modes = jnp.concatenate(ks * p.fold, axis=1)
    modes_ref[...] = modes
    rows = p.c // p.fold
    sums = jnp.zeros((rows, LANES), F32)
    for chip in range(p.chips):
        for core in range(2):
            tile = jnp.bitwise_xor(lax.div(place_ref[3], 2), chip) * 2 + jnp.bitwise_xor(place_ref[0], core)
            for o in range(p.own):
                w = cross_ref[chip, o] if core else w_refs[chip][0, o]
                sums = sums + w * modes_ref[pl.ds(tile * p.own + o, 1), :]
    down = sums.T
    pieces = []
    for k in range(p.per_row):
        for f in range(p.fold):
            start = (f * p.per_row + k) * p.slot
            pieces.append(down[start : start + p.slot, :])
    dual = jnp.concatenate(pieces, axis=1)
    parity = place_ref[0]
    for q in range(p.tiles // 2):
        even = modes[2 * q * p.own : (2 * q + 1) * p.own, :]
        odd = modes[(2 * q + 1) * p.own : (2 * q + 2) * p.own, :]
        mine = jnp.where(parity == 0, even, odd)
        other = jnp.where(parity == 0, odd, even)
        pieces = [mine, other]
        if 2 * p.own < SUB:
            pieces.append(jnp.zeros((SUB - 2 * p.own, LANES), F32))
        both = jnp.concatenate(pieces, axis=0)
        for g in range(p.groups):
            d = g * (p.tiles // 2) + q
            out_ref[d, : p.slot, :] = dual
            out_ref[d, p.slot :, :] = both


def grad_body(plan, got_ref, more_ref, saved_ref, out_ref):
    p = plan
    place_ref = place_of(p)
    base = place_ref[1] * (p.tiles // 2)
    parity = place_ref[0]
    lane = lax.broadcasted_iota(jnp.int32, (SUB, LANES), 1)
    source = lane % p.per_row * p.slot + lane % K // p.per_row * p.run + lane // K
    source = jnp.clip(source, 0, LANES - 1)
    pieces = []
    for q in range(p.tiles // 2):
        one = jnp.take_along_axis(got_ref[base + q, p.slot :, :], source, axis=1)[: p.own]
        two = jnp.take_along_axis(more_ref[base + q, p.slot :, :], source, axis=1)[p.own : 2 * p.own]
        for t, piece in (
            (2 * q, jnp.where(parity == 0, one, two)),
            (2 * q + 1, jnp.where(parity == 0, two, one)),
        ):
            if p.valid(t) > 0:
                pieces.append(piece[:, : p.valid(t) * K])
    spectrum = jnp.concatenate(pieces, axis=1)
    for o in range(p.own):
        out_ref[o] = saved_ref[...] * spectrum[o : o + 1, :]


def solution(mesh):
    def local(cotangent, deriv_two, deriv_one, point_two, point_one, modes_two, modes_one, saved_two, saved_one):
        shape = cotangent.shape
        channels = shape[1]
        plan = p = Plan(mesh, shape[2:], channels)
        xy = p.x * p.y

        full_x, full_y, full_z = basis(p.x * p.groups), basis(p.y * p.tiles), basis(p.z)
        rows_x, rows_y = [], []
        for parity in range(2):
            pair, used = [], []
            for h in (parity, 1 - parity):
                for d in range(p.half):
                    tile = d % (p.tiles // 2) * 2 + h
                    own = np.arange(p.run)
                    used.append(own < p.valid(tile))
                    start = d // (p.tiles // 2) * p.pairs + tile * p.run
                    pair.append(np.where(used[-1], start + own, 0))
            pair, used = np.concatenate(pair), np.concatenate(used)
            rows_x.append(full_x[pair // K] * used[:, None].astype(np.float32))
            rows_y.append(full_y[pair % K])
        rows_x = np.stack(rows_x).reshape(2, p.rows, p.groups, p.x).transpose(0, 2, 3, 1)
        rows_x = rows_x.reshape(2 * p.groups, p.x, p.rows)
        rows_y = np.stack(rows_y).reshape(2, p.rows, p.tiles // 2, 2, p.y)
        rows_y = np.stack([rows_y[h, :, :, h] for h in range(2)]).transpose(2, 0, 3, 1)
        rows_y = rows_y.reshape(p.tiles, p.y, p.rows)
        rows_x, rows_y = two_parts(rows_x), two_parts(rows_y)
        ex = jnp.asarray(np.tile(np.repeat(np.eye(p.x, dtype=np.float32), p.y, axis=1), (2, 1))).astype(BF16)
        ey = jnp.asarray(np.tile(np.eye(p.y, dtype=np.float32), (2, p.x))).astype(BF16)
        groups = p.c // p.step
        tz = np.zeros((LANES, p.step, p.z), np.float32)
        lines = np.zeros((K, groups, p.step, groups, LANES), np.float32)
        for u in range(p.step):
            for k in range(K):
                tz[k * p.step + u, u] = full_z[k]
                lines[k, np.arange(groups), u, np.arange(groups), k * p.step + u] = 1.0
        tz = jnp.asarray(tz.reshape(LANES, p.step * p.z)).astype(BF16)
        lines = jnp.asarray(lines.reshape(p.width, groups * LANES)).astype(BF16)
        spread = jnp.asarray(np.repeat(np.eye(p.c, dtype=np.float32), p.y, axis=0)).astype(BF16)

        target = np.full((p.chips, 1, p.tiles * p.lanes), -1, np.int32)
        for chip in range(p.chips):
            for tile in range(p.tiles):
                at = ((tile // 2 ^ chip) * 2 + tile % 2) * p.lanes
                for r in range(p.valid(tile)):
                    for k in range(K):
                        lane = k % p.per_row * p.slot + k // p.per_row * p.run + r
                        target[chip, 0, at + lane] = (tile * p.run + r) * K + k
        target = jnp.asarray(target)

        field = (p.c, xy, p.z)
        slots = (p.devices, p.slot, LANES)
        packed = (p.half, p.packed, LANES)
        g_scr = pltpu.VMEM((groups, xy, LANES), BF16)
        s_scr = pltpu.VMEM((p.rows, p.width), F32)
        modes_scr = g_scr
        blocked = pl.BlockSpec((p.step, xy, p.z), lambda n: (n, 0, 0))
        steps = (p.c // p.step,)
        partners = [(i, i ^ 1) for i in range(p.tiles)]
        same = [
            [e * p.tiles + 2 * q + h for e in range(p.groups) for q in range(p.tiles // 2)] for h in range(2)
        ]

        def in_hbm(array):
            return pltpu.with_memory_space_constraint(array, pltpu.HBM)

        block = (2, 2, p.own, p.c // p.fold, LANES)
        odd, *even = call(
            pack_body, p, [((p.chips // 2, *block), F32)] + [(block, F32)] * (p.chips // 2),
            [
                pltpu.VMEM((p.own, p.c, p.pairs * K), F32),
                pltpu.VMEM((p.own, p.c, p.pairs * K), F32),
                pltpu.VMEM(target.shape, jnp.int32),
                pltpu.VMEM((p.pairs * K, p.tiles * p.lanes), BF16),
                pltpu.SemaphoreType.DMA((3,)),
            ],
            specs=[HBM, HBM, HBM],
        )(in_hbm(modes_two.transpose(1, 2, 0)), in_hbm(modes_one.transpose(1, 2, 0)), in_hbm(target))

        def swap(blocks, bit):
            return lax.ppermute(blocks, "tile", [(i, i ^ (2 * bit)) for i in range(p.tiles)])

        got = swap(odd, 1)
        first = {(0, 2 * n): part for n, part in enumerate(even)}
        first |= {(1, 2 * n): got[n] for n in range(p.chips // 2)}

        def deal(layer):
            held = {key: part[:, layer] for key, part in first.items()}
            bit = 2
            while bit < p.chips:
                leaving = sorted(key for key in held if key[1] & bit)
                parts = jnp.stack([held.pop(key) for key in leaving])
                got = swap(parts, bit)
                held |= {(key[0] ^ bit, key[1] ^ bit): got[n] for n, key in enumerate(leaving)}
                bit *= 2
            dealt = [held[chip, 0] for chip in range(p.chips)]
            crossing = jnp.stack([part[1] for part in dealt])
            return (*dealt, lax.ppermute(crossing, "tile", partners))

        weights_two = deal(0)
        weights_one = deal(1)

        def exchange(parts):
            return lax.all_to_all(parts, BOTH, 0, 0, tiled=True, axis_index_groups=same)

        def partner(parts):
            return lax.ppermute(parts, "tile", partners)

        def dual(got, weights):
            return call(
                dual_body, p, [(packed, F32)], [pltpu.VMEM((p.c, LANES), F32)],
                count=p.chips + 2,
            )(got, *weights)[0]

        def pointwise(w, *factors):
            return call(
                pointwise_body, p, [(field, F32)], [pltpu.VMEM((p.c * p.y, p.c * p.y), BF16)],
                count=2 + len(factors),
            )(*factors, w, spread)[0]

        def grad(got, more, saved):
            out = call(grad_body, p, [((p.own, p.c, p.pairs * K), F32)], count=3)(got, more, saved[0].T)[0]
            return out.transpose(2, 0, 1)

        part_two, table, turned = call(
            analyse_body, p, [(slots, F32), ((2 * p.rows, xy), BF16), ((xy, p.rows), BF16)],
            [
                g_scr, s_scr, pltpu.VMEM(field, BF16), pltpu.VMEM((2 * p.rows, xy), BF16),
                pltpu.VMEM((xy, p.rows), BF16), pltpu.SemaphoreType.DMA((groups + 2,)),
            ],
            specs=[VMEM, HBM] + [VMEM] * 6, out_specs=[VMEM, HBM, HBM], grid=steps,
        )(cotangent.reshape(field), in_hbm(deriv_two.reshape(field)), tz, lines, rows_x, rows_y, ex, ey)
        got_two = lax.all_to_all(part_two, BOTH, 0, 0, tiled=True)
        point_out = pointwise(point_two, cotangent.reshape(field), deriv_two.reshape(field))
        share_two = dual(got_two, weights_two)
        all_two = exchange(share_two)
        more_two = partner(all_two)
        gated_one, part_one = call(
            synth_analyse_body, p, [(field, BF16), (slots, F32)], [
                g_scr, s_scr, s_scr, modes_scr, pltpu.VMEM(field, BF16), pltpu.VMEM(tz.shape, BF16),
                pltpu.VMEM(turned.shape, BF16), pltpu.VMEM(table.shape, BF16),
                pltpu.SemaphoreType.DMA(steps), pltpu.SemaphoreType.DMA((3,)),
            ],
            specs=[VMEM] * 5 + [HBM] * 3, out_specs=[HBM, VMEM], grid=steps,
        )(all_two, more_two, point_out, deriv_one.reshape(field), lines, in_hbm(tz), in_hbm(turned), in_hbm(table))
        got_one = lax.all_to_all(part_one, BOTH, 0, 0, tiled=True)
        grad_two = grad(all_two, more_two, saved_two)
        point_out = pointwise(point_one, gated_one)
        share_one = dual(got_one, weights_one)
        all_one = exchange(share_one)
        more_one = partner(all_one)
        result, grad_one = call(
            synth_body, p, [(field, BF16), ((p.own, p.c, p.pairs * K), F32)], [s_scr, modes_scr],
            specs=[VMEM] * 7,
            out_specs=[blocked, pl.BlockSpec((p.own, p.c, p.pairs * K), lambda n: (0, 0, 0))],
            grid=steps,
        )(all_one, more_one, point_out, tz, lines, turned, saved_one[0].T)
        grad_one = grad_one.transpose(2, 0, 1)
        return (result.reshape(shape), grad_one, grad_two)

    return jax.shard_map(
        local,
        mesh=mesh,
        in_specs=(
            P(None, None, "grp", "tile", None),
            P(None, None, "grp", "tile", None),
            P(None, None, "grp", "tile", None),
            P(),
            P(),
            P("grp", "tile", None),
            P("grp", "tile", None),
            P(None, "grp", None),
            P(None, "grp", None),
        ),
        out_specs=(
            P(None, None, "grp", "tile", None),
            P("grp", "tile", None),
            P("grp", "tile", None),
        ),
        check_vma=False,
    )
```

```python
import functools
import math

import jax
import jax.numpy as jnp
import numpy as np
from jax import lax
from jax.experimental import pallas as pl
from jax.experimental.pallas import tpu as pltpu
from jax.sharding import PartitionSpec as P


K = 12
LANES = 128
SUB = 8
COST = 1 << 31
BOTH = ("grp", "tile")
VMEM = pl.BlockSpec(memory_space=pltpu.VMEM)
HBM = pl.BlockSpec(memory_space=pltpu.HBM)
F32 = jnp.float32
BF16 = jnp.bfloat16


def basis(length):
    position = np.arange(length)
    orders = np.arange(K)
    frequency = (orders + 1) // 2
    phase = frequency[:, None] * position[None, :] % length
    angle = 2.0 * math.pi / length * phase
    factor = math.sqrt(2.0 / length)
    values = np.where(orders[:, None] % 2 == 1, factor * np.cos(angle), factor * np.sin(angle))
    values[0] = 1.0 / math.sqrt(length)
    return values.astype(np.float32)


def place_of(plan):
    group, tile = lax.axis_index("grp"), lax.axis_index("tile")
    parity = jnp.bitwise_and(tile, 1)
    return parity, group, parity * plan.groups + group, tile


def two_parts(table):
    high = table.astype(jnp.bfloat16)
    return jnp.asarray(np.concatenate([high, (table - high.astype(np.float32)).astype(jnp.bfloat16)], axis=1))


class Plan:
    def __init__(self, mesh, cells, channels):
        self.groups, self.tiles = mesh.shape["grp"], mesh.shape["tile"]
        self.devices = self.groups * self.tiles
        self.x, self.y, self.z = cells
        self.c = channels
        self.per_row = LANES // channels
        self.blocks = K // self.per_row
        self.width = K * channels
        self.pairs = K * K // self.groups
        self.run = -(-self.pairs // self.tiles)
        self.slot = -(-self.run * self.blocks // SUB) * SUB
        self.packed = self.slot + SUB
        self.half = self.devices // 2
        self.chips = self.tiles // 2
        self.lanes = self.per_row * self.slot
        self.fold = LANES // self.lanes
        self.rows = self.devices * self.run
        self.own = channels // self.tiles
        self.step = 8

    def valid(self, tile):
        return max(0, min(self.run, self.pairs - self.run * tile))


def call(body, plan, outs, scratch=(), specs=None, out_specs=None, count=None, limit=8, grid=()):
    return pl.pallas_call(
        functools.partial(body, plan),
        grid=grid,
        out_shape=tuple(
            pltpu.HBM(s, d) if spec is not VMEM else jax.ShapeDtypeStruct(s, d)
            for (s, d), spec in zip(outs, out_specs or [VMEM] * len(outs))
        ),
        in_specs=specs or [VMEM] * count,
        out_specs=tuple(out_specs or [VMEM] * len(outs)),
        scratch_shapes=list(scratch),
        compiler_params=pltpu.CompilerParams(vmem_limit_bytes=limit << 20),
        cost_estimate=pl.CostEstimate(flops=COST, bytes_accessed=COST // 1000, transcendentals=0),
    )


def emit_slots(plan, g_ref, order_ref, table_ref, slots_ref, s_ref):
    p = plan
    place_ref = place_of(p)
    lines = jnp.concatenate([g_ref[n] for n in range(p.c // p.step)], axis=1)
    lines = lax.dot_general(lines, order_ref[...], (((1,), (1,)), ((), ())), preferred_element_type=F32).astype(BF16)
    both = jnp.dot(table_ref[...], lines, preferred_element_type=F32)
    s_ref[...] = both[: p.rows] + both[p.rows :]
    for d in range(p.devices):
        parity = place_ref[0] if d < p.half else 1 - place_ref[0]
        n = (d % p.half // p.chips) * p.tiles + d % p.chips * 2 + parity
        for j in range(p.blocks):
            slots_ref[n, j * p.run : (j + 1) * p.run, :] = s_ref[
                d * p.run : (d + 1) * p.run, j * LANES : (j + 1) * LANES
            ]
        if p.blocks * p.run < p.slot:
            slots_ref[n, p.blocks * p.run :, :] = jnp.zeros((p.slot - p.blocks * p.run, LANES), F32)


def product(up, der):
    return (up.astype(F32) * der.astype(F32)).astype(BF16)


def spread_rows(rows, cells):
    return lax.dot_general(rows, cells, (((0,), (0,)), ((), ())), preferred_element_type=F32)


def analyse_body(
    plan, up_ref, der_hbm, tz_ref, order_ref, rx_ref, ry_ref, ex_ref, ey_ref,
    slots_ref, table_hbm, turned_hbm, g_ref, s_ref, der_ref, table_ref, turned_ref, sems,
):
    p = plan
    place_ref = place_of(p)
    step = pl.program_id(0)

    def fetch(n):
        part = pl.ds(n * p.step, p.step)
        return pltpu.make_async_copy(der_hbm.at[part], der_ref.at[part], sems.at[n])

    last = p.c // p.step
    tables = (
        pltpu.make_async_copy(table_ref, table_hbm, sems.at[last]),
        pltpu.make_async_copy(turned_ref, turned_hbm, sems.at[last + 1]),
    )

    @pl.when(step == 0)
    def _():
        for n in range(p.c // p.step):
            fetch(n).start()
        table = spread_rows(rx_ref[place_ref[2]], ex_ref[...]) * spread_rows(ry_ref[place_ref[3]], ey_ref[...])
        high = table.astype(BF16)
        table_ref[: p.rows] = high
        table_ref[p.rows :] = (table - high.astype(F32)).astype(BF16)
        turned_ref[...] = table.T.astype(BF16)
        for copy in tables:
            copy.start()

    first = step * p.step
    fetch(step).wait()
    parts = [product(up_ref[first + u], der_ref[first + u]) for u in range(p.step)]
    g_ref[step] = lax.dot_general(
        jnp.concatenate(parts, axis=1), tz_ref[...], (((1,), (1,)), ((), ())), preferred_element_type=F32
    ).astype(BF16)

    @pl.when(step == pl.num_programs(0) - 1)
    def _():
        emit_slots(p, g_ref, order_ref, table_ref, slots_ref, s_ref)
        for copy in tables:
            copy.wait()


def gather_modes(plan, got_ref, more_ref, order_ref, turned_ref, d_ref, modes_ref):
    p = plan
    for d in range(p.devices):
        from_ref, n = (got_ref, d) if d < p.half else (more_ref, d - p.half)
        for j in range(p.blocks):
            d_ref[d * p.run : (d + 1) * p.run, j * LANES : (j + 1) * LANES] = from_ref[
                n, j * p.run : (j + 1) * p.run, :
            ]
    lines = jnp.dot(turned_ref[...], d_ref[...].astype(BF16), preferred_element_type=F32).astype(BF16)
    lines = jnp.dot(lines, order_ref[...], preferred_element_type=F32).astype(BF16)
    for n in range(p.c // p.step):
        modes_ref[n] = lines[:, n * LANES : (n + 1) * LANES]


def synth_analyse_body(
    plan, got_ref, more_ref, point_ref, der_ref, order_ref, tz_ref, turned_ref, table_ref,
    gated_ref, slots_ref, g_ref, s_ref, d_ref, modes_ref, field_ref, sems,
):
    p = plan
    step = pl.program_id(0)

    def store(n):
        part = pl.ds(n * p.step, p.step)
        return pltpu.make_async_copy(field_ref.at[part], gated_ref.at[part], sems.at[n])

    @pl.when(step == 0)
    def _():
        gather_modes(p, got_ref, more_ref, order_ref, turned_ref, d_ref, modes_ref)

    first = step * p.step
    synth = jnp.dot(modes_ref[step], tz_ref[...], preferred_element_type=F32)
    parts = []
    for u in range(p.step):
        middle = (point_ref[first + u].astype(F32) + synth[:, u * p.z : (u + 1) * p.z]).astype(BF16)
        gated = product(middle, der_ref[first + u])
        field_ref[first + u] = gated
        parts.append(gated)
    store(step).start()
    g_ref[step] = lax.dot_general(
        jnp.concatenate(parts, axis=1), tz_ref[...], (((1,), (1,)), ((), ())), preferred_element_type=F32
    ).astype(BF16)

    @pl.when(step == pl.num_programs(0) - 1)
    def _():
        emit_slots(p, g_ref, order_ref, table_ref, slots_ref, s_ref)
        for n in range(p.c // p.step):
            store(n).wait()


def synth_body(
    plan, got_ref, more_ref, point_ref, tz_ref, order_ref, turned_ref, saved_ref, out_ref, grad_ref,
    d_ref, modes_ref,
):
    p = plan
    step = pl.program_id(0)

    @pl.when(step == 0)
    def _():
        gather_modes(p, got_ref, more_ref, order_ref, turned_ref, d_ref, modes_ref)
        grad_body(p, got_ref, more_ref, saved_ref, grad_ref)

    first = step * p.step
    synth = jnp.dot(modes_ref[step], tz_ref[...], preferred_element_type=F32)
    for u in range(p.step):
        out_ref[u] = (point_ref[first + u].astype(F32) + synth[:, u * p.z : (u + 1) * p.z]).astype(BF16)


def pointwise_body(plan, *refs):
    p = plan
    *field_refs, w_ref, spread_ref, out_ref, big_ref = refs
    n = p.c * p.y
    spread = spread_ref[...]
    rows = lax.dot_general(spread, w_ref[...], (((1,), (1,)), ((), ())), preferred_element_type=F32).astype(BF16)
    both = lax.dot_general(rows, spread, (((1,), (1,)), ((), ())), preferred_element_type=F32)
    same = (
        lax.broadcasted_iota(jnp.int32, (n, n), 0) % p.y == lax.broadcasted_iota(jnp.int32, (n, n), 1) % p.y
    )
    big_ref[...] = jnp.where(same, both, 0.0).astype(BF16)
    for x in range(0, p.x, 2):
        pair = []
        for h in range(2):
            cells = [ref[:, (x + h) * p.y : (x + h + 1) * p.y, :] for ref in field_refs]
            pair.append((product(*cells) if len(cells) == 2 else cells[0]).reshape(n, p.z))
        out = jnp.dot(big_ref[...], jnp.concatenate(pair, axis=1), preferred_element_type=F32)
        for h in range(2):
            out_ref[:, (x + h) * p.y : (x + h + 1) * p.y, :] = (
                out[:, h * p.z : (h + 1) * p.z].astype(BF16).reshape(p.c, p.y, p.z)
            )


def pack_body(plan, two_hbm, one_hbm, target_hbm, odd_ref, *refs):
    p = plan
    place_ref = place_of(p)
    *even_refs, two_ref, one_ref, target_ref, order_ref, sems = refs
    n = p.own * p.c
    rows = p.c // p.fold
    copies = [
        pltpu.make_async_copy(two_hbm, two_ref, sems.at[0]),
        pltpu.make_async_copy(one_hbm, one_ref, sems.at[1]),
        pltpu.make_async_copy(target_hbm, target_ref, sems.at[2]),
    ]
    for copy in (copies[2], *copies[:2]):
        copy.start()
    copies[2].wait()
    mode = lax.broadcasted_iota(jnp.int32, order_ref.shape, 0)
    order_ref[...] = jnp.where(mode == target_ref[lax.div(place_ref[3], 2)], 1.0, 0.0).astype(BF16)
    for layer, w_ref in enumerate((two_ref, one_ref)):
        copies[layer].wait()
        rest = w_ref[...].reshape(n, p.pairs * K)
        parts = []
        for _ in range(2):
            parts.append(rest.astype(BF16))
            rest = rest - parts[-1].astype(F32)
        moved = jnp.dot(jnp.concatenate(parts, axis=0), order_ref[...], preferred_element_type=F32)
        moved = moved[:n] + moved[n:]
        for o in range(p.own):
            mine = moved[o * p.c : (o + 1) * p.c]
            for t in range(p.tiles):
                core = jnp.bitwise_xor(place_ref[0], t % 2)
                chip = t // 2
                block = jnp.concatenate(
                    [mine[f * rows : (f + 1) * rows, t * p.lanes : (t + 1) * p.lanes] for f in range(p.fold)], axis=1
                )
                if chip % 2:
                    odd_ref[chip // 2, core, layer, o] = block
                else:
                    even_refs[chip // 2][core, layer, o] = block


def dual_body(plan, got_ref, *refs):
    p = plan
    place_ref = place_of(p)
    w_refs, cross_ref, out_ref, modes_ref = refs[: p.chips], *refs[p.chips :]
    total = got_ref[0]
    for d in range(1, p.devices):
        total = total + got_ref[d]
    down = total.T
    ks = [down[k * p.c : (k + 1) * p.c, :] for k in range(p.per_row)]
    modes = jnp.concatenate(ks * p.fold, axis=1)
    modes_ref[...] = modes
    rows = p.c // p.fold
    sums = jnp.zeros((rows, LANES), F32)
    for chip in range(p.chips):
        for core in range(2):
            tile = jnp.bitwise_xor(lax.div(place_ref[3], 2), chip) * 2 + jnp.bitwise_xor(place_ref[0], core)
            for o in range(p.own):
                w = cross_ref[chip, o] if core else w_refs[chip][0, o]
                sums = sums + w * modes_ref[pl.ds(tile * p.own + o, 1), :]
    down = sums.T
    pieces = []
    for k in range(p.per_row):
        for f in range(p.fold):
            start = (f * p.per_row + k) * p.slot
            pieces.append(down[start : start + p.slot, :])
    dual = jnp.concatenate(pieces, axis=1)
    parity = place_ref[0]
    for q in range(p.tiles // 2):
        even = modes[2 * q * p.own : (2 * q + 1) * p.own, :]
        odd = modes[(2 * q + 1) * p.own : (2 * q + 2) * p.own, :]
        mine = jnp.where(parity == 0, even, odd)
        other = jnp.where(parity == 0, odd, even)
        pieces = [mine, other]
        if 2 * p.own < SUB:
            pieces.append(jnp.zeros((SUB - 2 * p.own, LANES), F32))
        both = jnp.concatenate(pieces, axis=0)
        for g in range(p.groups):
            d = g * (p.tiles // 2) + q
            out_ref[d, : p.slot, :] = dual
            out_ref[d, p.slot :, :] = both


def grad_body(plan, got_ref, more_ref, saved_ref, out_ref):
    p = plan
    place_ref = place_of(p)
    base = place_ref[1] * (p.tiles // 2)
    parity = place_ref[0]
    lane = lax.broadcasted_iota(jnp.int32, (SUB, LANES), 1)
    source = lane % p.per_row * p.slot + lane % K // p.per_row * p.run + lane // K
    source = jnp.clip(source, 0, LANES - 1)
    pieces = []
    for q in range(p.tiles // 2):
        one = jnp.take_along_axis(got_ref[base + q, p.slot :, :], source, axis=1)[: p.own]
        two = jnp.take_along_axis(more_ref[base + q, p.slot :, :], source, axis=1)[p.own : 2 * p.own]
        for t, piece in (
            (2 * q, jnp.where(parity == 0, one, two)),
            (2 * q + 1, jnp.where(parity == 0, two, one)),
        ):
            if p.valid(t) > 0:
                pieces.append(piece[:, : p.valid(t) * K])
    spectrum = jnp.concatenate(pieces, axis=1)
    for o in range(p.own):
        out_ref[o] = saved_ref[...] * spectrum[o : o + 1, :]


def solution(mesh):
    def local(cotangent, deriv_two, deriv_one, point_two, point_one, modes_two, modes_one, saved_two, saved_one):
        shape = cotangent.shape
        channels = shape[1]
        plan = p = Plan(mesh, shape[2:], channels)
        xy = p.x * p.y

        full_x, full_y, full_z = basis(p.x * p.groups), basis(p.y * p.tiles), basis(p.z)
        rows_x, rows_y = [], []
        for parity in range(2):
            pair, used = [], []
            for h in (parity, 1 - parity):
                for d in range(p.half):
                    tile = d % (p.tiles // 2) * 2 + h
                    own = np.arange(p.run)
                    used.append(own < p.valid(tile))
                    start = d // (p.tiles // 2) * p.pairs + tile * p.run
                    pair.append(np.where(used[-1], start + own, 0))
            pair, used = np.concatenate(pair), np.concatenate(used)
            rows_x.append(full_x[pair // K] * used[:, None].astype(np.float32))
            rows_y.append(full_y[pair % K])
        rows_x = np.stack(rows_x).reshape(2, p.rows, p.groups, p.x).transpose(0, 2, 3, 1)
        rows_x = rows_x.reshape(2 * p.groups, p.x, p.rows)
        rows_y = np.stack(rows_y).reshape(2, p.rows, p.tiles // 2, 2, p.y)
        rows_y = np.stack([rows_y[h, :, :, h] for h in range(2)]).transpose(2, 0, 3, 1)
        rows_y = rows_y.reshape(p.tiles, p.y, p.rows)
        rows_x, rows_y = two_parts(rows_x), two_parts(rows_y)
        ex = jnp.asarray(np.tile(np.repeat(np.eye(p.x, dtype=np.float32), p.y, axis=1), (2, 1))).astype(BF16)
        ey = jnp.asarray(np.tile(np.eye(p.y, dtype=np.float32), (2, p.x))).astype(BF16)
        groups = p.c // p.step
        tz = np.zeros((LANES, p.step, p.z), np.float32)
        lines = np.zeros((K, groups, p.step, groups, LANES), np.float32)
        for u in range(p.step):
            for k in range(K):
                tz[k * p.step + u, u] = full_z[k]
                lines[k, np.arange(groups), u, np.arange(groups), k * p.step + u] = 1.0
        tz = jnp.asarray(tz.reshape(LANES, p.step * p.z)).astype(BF16)
        lines = jnp.asarray(lines.reshape(p.width, groups * LANES)).astype(BF16)
        spread = jnp.asarray(np.repeat(np.eye(p.c, dtype=np.float32), p.y, axis=0)).astype(BF16)

        target = np.full((p.chips, 1, p.tiles * p.lanes), -1, np.int32)
        for chip in range(p.chips):
            for tile in range(p.tiles):
                at = ((tile // 2 ^ chip) * 2 + tile % 2) * p.lanes
                for r in range(p.valid(tile)):
                    for k in range(K):
                        lane = k % p.per_row * p.slot + k // p.per_row * p.run + r
                        target[chip, 0, at + lane] = (tile * p.run + r) * K + k
        target = jnp.asarray(target)

        field = (p.c, xy, p.z)
        slots = (p.devices, p.slot, LANES)
        packed = (p.half, p.packed, LANES)
        g_scr = pltpu.VMEM((groups, xy, LANES), BF16)
        s_scr = pltpu.VMEM((p.rows, p.width), F32)
        modes_scr = g_scr
        blocked = pl.BlockSpec((p.step, xy, p.z), lambda n: (n, 0, 0))
        steps = (p.c // p.step,)
        partners = [(i, i ^ 1) for i in range(p.tiles)]
        same = [
            [e * p.tiles + 2 * q + h for e in range(p.groups) for q in range(p.tiles // 2)] for h in range(2)
        ]

        def in_hbm(array):
            return pltpu.with_memory_space_constraint(array, pltpu.HBM)

        block = (2, 2, p.own, p.c // p.fold, LANES)
        odd, *even = call(
            pack_body, p, [((p.chips // 2, *block), F32)] + [(block, F32)] * (p.chips // 2),
            [
                pltpu.VMEM((p.own, p.c, p.pairs * K), F32),
                pltpu.VMEM((p.own, p.c, p.pairs * K), F32),
                pltpu.VMEM(target.shape, jnp.int32),
                pltpu.VMEM((p.pairs * K, p.tiles * p.lanes), BF16),
                pltpu.SemaphoreType.DMA((3,)),
            ],
            specs=[HBM, HBM, HBM],
        )(in_hbm(modes_two.transpose(1, 2, 0)), in_hbm(modes_one.transpose(1, 2, 0)), in_hbm(target))

        def swap(blocks, bit):
            return lax.ppermute(blocks, "tile", [(i, i ^ (2 * bit)) for i in range(p.tiles)])

        got = swap(odd, 1)
        first = {(0, 2 * n): part for n, part in enumerate(even)}
        first |= {(1, 2 * n): got[n] for n in range(p.chips // 2)}

        def deal(layer):
            held = {key: part[:, layer] for key, part in first.items()}
            bit = 2
            while bit < p.chips:
                leaving = sorted(key for key in held if key[1] & bit)
                parts = jnp.stack([held.pop(key) for key in leaving])
                got = swap(parts, bit)
                held |= {(key[0] ^ bit, key[1] ^ bit): got[n] for n, key in enumerate(leaving)}
                bit *= 2
            dealt = [held[chip, 0] for chip in range(p.chips)]
            crossing = jnp.stack([part[1] for part in dealt])
            return (*dealt, lax.ppermute(crossing, "tile", partners))

        weights_two = deal(0)
        weights_one = deal(1)

        def exchange(parts):
            return lax.all_to_all(parts, BOTH, 0, 0, tiled=True, axis_index_groups=same)

        def partner(parts):
            return lax.ppermute(parts, "tile", partners)

        def dual(got, weights):
            return call(
                dual_body, p, [(packed, F32)], [pltpu.VMEM((p.c, LANES), F32)],
                count=p.chips + 2,
            )(got, *weights)[0]

        def pointwise(w, *factors):
            return call(
                pointwise_body, p, [(field, BF16)], [pltpu.VMEM((p.c * p.y, p.c * p.y), BF16)],
                count=2 + len(factors),
            )(*factors, w, spread)[0]

        def grad(got, more, saved):
            out = call(grad_body, p, [((p.own, p.c, p.pairs * K), F32)], count=3)(got, more, saved[0].T)[0]
            return out.transpose(2, 0, 1)

        part_two, table, turned = call(
            analyse_body, p, [(slots, F32), ((2 * p.rows, xy), BF16), ((xy, p.rows), BF16)],
            [
                g_scr, s_scr, pltpu.VMEM(field, BF16), pltpu.VMEM((2 * p.rows, xy), BF16),
                pltpu.VMEM((xy, p.rows), BF16), pltpu.SemaphoreType.DMA((groups + 2,)),
            ],
            specs=[VMEM, HBM] + [VMEM] * 6, out_specs=[VMEM, HBM, HBM], grid=steps,
        )(cotangent.reshape(field), in_hbm(deriv_two.reshape(field)), tz, lines, rows_x, rows_y, ex, ey)
        got_two = lax.all_to_all(part_two, BOTH, 0, 0, tiled=True)
        point_out = pointwise(point_two, cotangent.reshape(field), deriv_two.reshape(field))
        share_two = dual(got_two, weights_two)
        all_two = exchange(share_two)
        more_two = partner(all_two)
        gated_one, part_one = call(
            synth_analyse_body, p, [(field, BF16), (slots, F32)], [
                g_scr, s_scr, s_scr, modes_scr, pltpu.VMEM(field, BF16), pltpu.SemaphoreType.DMA(steps),
            ],
            count=8, out_specs=[HBM, VMEM], grid=steps,
        )(all_two, more_two, point_out, deriv_one.reshape(field), lines, tz, turned, table)
        got_one = lax.all_to_all(part_one, BOTH, 0, 0, tiled=True)
        grad_two = grad(all_two, more_two, saved_two)
        point_out = pointwise(point_one, gated_one)
        share_one = dual(got_one, weights_one)
        all_one = exchange(share_one)
        more_one = partner(all_one)
        result, grad_one = call(
            synth_body, p, [(field, BF16), ((p.own, p.c, p.pairs * K), F32)], [s_scr, modes_scr],
            specs=[VMEM] * 7,
            out_specs=[blocked, pl.BlockSpec((p.own, p.c, p.pairs * K), lambda n: (0, 0, 0))],
            grid=steps,
        )(all_one, more_one, point_out, tz, lines, turned, saved_one[0].T)
        grad_one = grad_one.transpose(2, 0, 1)
        return (result.reshape(shape), grad_one, grad_two)

    return jax.shard_map(
        local,
        mesh=mesh,
        in_specs=(
            P(None, None, "grp", "tile", None),
            P(None, None, "grp", "tile", None),
            P(None, None, "grp", "tile", None),
            P(),
            P(),
            P("grp", "tile", None),
            P("grp", "tile", None),
            P(None, "grp", None),
            P(None, "grp", None),
        ),
        out_specs=(
            P(None, None, "grp", "tile", None),
            P("grp", "tile", None),
            P("grp", "tile", None),
        ),
        check_vma=False,
    )
```

```python
import functools
import math

import jax
import jax.numpy as jnp
import numpy as np
from jax import lax
from jax.experimental import pallas as pl
from jax.experimental.pallas import tpu as pltpu
from jax.sharding import PartitionSpec as P


K = 12
LANES = 128
SUB = 8
COST = 1 << 31
BOTH = ("grp", "tile")
VMEM = pl.BlockSpec(memory_space=pltpu.VMEM)
HBM = pl.BlockSpec(memory_space=pltpu.HBM)
F32 = jnp.float32
BF16 = jnp.bfloat16


def basis(length):
    position = np.arange(length)
    orders = np.arange(K)
    frequency = (orders + 1) // 2
    phase = frequency[:, None] * position[None, :] % length
    angle = 2.0 * math.pi / length * phase
    factor = math.sqrt(2.0 / length)
    values = np.where(orders[:, None] % 2 == 1, factor * np.cos(angle), factor * np.sin(angle))
    values[0] = 1.0 / math.sqrt(length)
    return values.astype(np.float32)


def place_of(plan):
    group, tile = lax.axis_index("grp"), lax.axis_index("tile")
    parity = jnp.bitwise_and(tile, 1)
    return parity, group, parity * plan.groups + group, tile


def two_parts(table):
    high = table.astype(jnp.bfloat16)
    return jnp.asarray(np.concatenate([high, (table - high.astype(np.float32)).astype(jnp.bfloat16)], axis=1))


class Plan:
    def __init__(self, mesh, cells, channels):
        self.groups, self.tiles = mesh.shape["grp"], mesh.shape["tile"]
        self.devices = self.groups * self.tiles
        self.x, self.y, self.z = cells
        self.c = channels
        self.per_row = LANES // channels
        self.blocks = K // self.per_row
        self.width = K * channels
        self.pairs = K * K // self.groups
        self.run = -(-self.pairs // self.tiles)
        self.slot = -(-self.run * self.blocks // SUB) * SUB
        self.packed = self.slot + SUB
        self.half = self.devices // 2
        self.chips = self.tiles // 2
        self.lanes = self.per_row * self.slot
        self.fold = LANES // self.lanes
        self.rows = self.devices * self.run
        self.own = channels // self.tiles
        self.step = 8

    def valid(self, tile):
        return max(0, min(self.run, self.pairs - self.run * tile))


def call(body, plan, outs, scratch=(), specs=None, out_specs=None, count=None, limit=8, grid=()):
    return pl.pallas_call(
        functools.partial(body, plan),
        grid=grid,
        out_shape=tuple(
            pltpu.HBM(s, d) if spec is not VMEM else jax.ShapeDtypeStruct(s, d)
            for (s, d), spec in zip(outs, out_specs or [VMEM] * len(outs))
        ),
        in_specs=specs or [VMEM] * count,
        out_specs=tuple(out_specs or [VMEM] * len(outs)),
        scratch_shapes=list(scratch),
        compiler_params=pltpu.CompilerParams(vmem_limit_bytes=limit << 20),
        cost_estimate=pl.CostEstimate(flops=COST, bytes_accessed=COST // 1000, transcendentals=0),
    )


def emit_slots(plan, g_ref, order_ref, table_ref, slots_ref, s_ref):
    p = plan
    place_ref = place_of(p)
    lines = jnp.concatenate([g_ref[n] for n in range(p.c // p.step)], axis=1)
    lines = lax.dot_general(lines, order_ref[...], (((1,), (1,)), ((), ())), preferred_element_type=F32).astype(BF16)
    both = jnp.dot(table_ref[...], lines, preferred_element_type=F32)
    s_ref[...] = both[: p.rows] + both[p.rows :]
    for d in range(p.devices):
        parity = place_ref[0] if d < p.half else 1 - place_ref[0]
        n = (d % p.half // p.chips) * p.tiles + d % p.chips * 2 + parity
        for j in range(p.blocks):
            slots_ref[n, j * p.run : (j + 1) * p.run, :] = s_ref[
                d * p.run : (d + 1) * p.run, j * LANES : (j + 1) * LANES
            ]
        if p.blocks * p.run < p.slot:
            slots_ref[n, p.blocks * p.run :, :] = jnp.zeros((p.slot - p.blocks * p.run, LANES), F32)


def product(up, der):
    return (up.astype(F32) * der.astype(F32)).astype(BF16)


def spread_rows(rows, cells):
    return lax.dot_general(rows, cells, (((0,), (0,)), ((), ())), preferred_element_type=F32)


def analyse_body(
    plan, up_ref, der_hbm, tz_ref, order_ref, rx_ref, ry_ref, ex_ref, ey_ref,
    slots_ref, table_hbm, turned_hbm, g_ref, s_ref, der_ref, table_ref, turned_ref, sems,
):
    p = plan
    place_ref = place_of(p)
    step = pl.program_id(0)

    def fetch(n):
        part = pl.ds(n * p.step, p.step)
        return pltpu.make_async_copy(der_hbm.at[part], der_ref.at[part], sems.at[n])

    last = p.c // p.step
    tables = (
        pltpu.make_async_copy(table_ref, table_hbm, sems.at[last]),
        pltpu.make_async_copy(turned_ref, turned_hbm, sems.at[last + 1]),
    )

    @pl.when(step == 0)
    def _():
        for n in range(p.c // p.step):
            fetch(n).start()
        table = spread_rows(rx_ref[place_ref[2]], ex_ref[...]) * spread_rows(ry_ref[place_ref[3]], ey_ref[...])
        high = table.astype(BF16)
        table_ref[: p.rows] = high
        table_ref[p.rows :] = (table - high.astype(F32)).astype(BF16)
        turned_ref[...] = table.T.astype(BF16)
        for copy in tables:
            copy.start()

    first = step * p.step
    fetch(step).wait()
    parts = [product(up_ref[first + u], der_ref[first + u]) for u in range(p.step)]
    g_ref[step] = lax.dot_general(
        jnp.concatenate(parts, axis=1), tz_ref[...], (((1,), (1,)), ((), ())), preferred_element_type=F32
    ).astype(BF16)

    @pl.when(step == pl.num_programs(0) - 1)
    def _():
        emit_slots(p, g_ref, order_ref, table_ref, slots_ref, s_ref)
        for copy in tables:
            copy.wait()


def gather_modes(plan, got_ref, more_ref, order_ref, turned_ref, d_ref, modes_ref):
    p = plan
    for d in range(p.devices):
        from_ref, n = (got_ref, d) if d < p.half else (more_ref, d - p.half)
        for j in range(p.blocks):
            d_ref[d * p.run : (d + 1) * p.run, j * LANES : (j + 1) * LANES] = from_ref[
                n, j * p.run : (j + 1) * p.run, :
            ]
    lines = jnp.dot(turned_ref[...], d_ref[...].astype(BF16), preferred_element_type=F32).astype(BF16)
    lines = jnp.dot(lines, order_ref[...], preferred_element_type=F32).astype(BF16)
    for n in range(p.c // p.step):
        modes_ref[n] = lines[:, n * LANES : (n + 1) * LANES]


def synth_analyse_body(
    plan, got_ref, more_ref, point_ref, der_ref, order_ref, tz_ref, turned_ref, table_ref,
    gated_ref, slots_ref, g_ref, s_ref, d_ref, modes_ref, field_ref, sems,
):
    p = plan
    step = pl.program_id(0)

    def store(n):
        part = pl.ds(n * p.step, p.step)
        return pltpu.make_async_copy(field_ref.at[part], gated_ref.at[part], sems.at[n])

    @pl.when(step == 0)
    def _():
        gather_modes(p, got_ref, more_ref, order_ref, turned_ref, d_ref, modes_ref)

    first = step * p.step
    synth = jnp.dot(modes_ref[step], tz_ref[...], preferred_element_type=F32)
    parts = []
    for u in range(p.step):
        middle = (point_ref[first + u].astype(F32) + synth[:, u * p.z : (u + 1) * p.z]).astype(BF16)
        gated = product(middle, der_ref[first + u])
        field_ref[first + u] = gated
        parts.append(gated)
    store(step).start()
    g_ref[step] = lax.dot_general(
        jnp.concatenate(parts, axis=1), tz_ref[...], (((1,), (1,)), ((), ())), preferred_element_type=F32
    ).astype(BF16)

    @pl.when(step == pl.num_programs(0) - 1)
    def _():
        emit_slots(p, g_ref, order_ref, table_ref, slots_ref, s_ref)
        for n in range(p.c // p.step):
            store(n).wait()


def synth_body(
    plan, got_ref, more_ref, point_ref, tz_ref, order_ref, turned_ref, saved_ref, out_ref, grad_hbm,
    d_ref, modes_ref, grad_ref, sem,
):
    p = plan
    step = pl.program_id(0)
    leaving = pltpu.make_async_copy(grad_ref, grad_hbm, sem.at[0])

    @pl.when(step == 0)
    def _():
        grad_body(p, got_ref, more_ref, saved_ref, grad_ref)
        leaving.start()
        gather_modes(p, got_ref, more_ref, order_ref, turned_ref, d_ref, modes_ref)

    first = step * p.step
    synth = jnp.dot(modes_ref[step], tz_ref[...], preferred_element_type=F32)
    for u in range(p.step):
        out_ref[u] = (point_ref[first + u].astype(F32) + synth[:, u * p.z : (u + 1) * p.z]).astype(BF16)

    @pl.when(step == pl.num_programs(0) - 1)
    def _():
        leaving.wait()


def pointwise_body(plan, *refs):
    p = plan
    *field_refs, w_ref, spread_ref, out_ref, big_ref = refs
    n = p.c * p.y
    spread = spread_ref[...]
    rows = lax.dot_general(spread, w_ref[...], (((1,), (1,)), ((), ())), preferred_element_type=F32).astype(BF16)
    both = lax.dot_general(rows, spread, (((1,), (1,)), ((), ())), preferred_element_type=F32)
    same = (
        lax.broadcasted_iota(jnp.int32, (n, n), 0) % p.y == lax.broadcasted_iota(jnp.int32, (n, n), 1) % p.y
    )
    big_ref[...] = jnp.where(same, both, 0.0).astype(BF16)
    for x in range(0, p.x, 2):
        pair = []
        for h in range(2):
            cells = [ref[:, (x + h) * p.y : (x + h + 1) * p.y, :] for ref in field_refs]
            pair.append((product(*cells) if len(cells) == 2 else cells[0]).reshape(n, p.z))
        out = jnp.dot(big_ref[...], jnp.concatenate(pair, axis=1), preferred_element_type=F32)
        for h in range(2):
            out_ref[:, (x + h) * p.y : (x + h + 1) * p.y, :] = (
                out[:, h * p.z : (h + 1) * p.z].astype(BF16).reshape(p.c, p.y, p.z)
            )


def pack_body(plan, two_hbm, one_hbm, target_hbm, odd_ref, *refs):
    p = plan
    place_ref = place_of(p)
    *even_refs, two_ref, one_ref, target_ref, order_ref, sems = refs
    n = p.own * p.c
    rows = p.c // p.fold
    copies = [
        pltpu.make_async_copy(two_hbm, two_ref, sems.at[0]),
        pltpu.make_async_copy(one_hbm, one_ref, sems.at[1]),
        pltpu.make_async_copy(target_hbm, target_ref, sems.at[2]),
    ]
    for copy in (copies[2], *copies[:2]):
        copy.start()
    copies[2].wait()
    mode = lax.broadcasted_iota(jnp.int32, order_ref.shape, 0)
    order_ref[...] = jnp.where(mode == target_ref[lax.div(place_ref[3], 2)], 1.0, 0.0).astype(BF16)
    for layer, w_ref in enumerate((two_ref, one_ref)):
        copies[layer].wait()
        rest = w_ref[...].reshape(n, p.pairs * K)
        parts = []
        for _ in range(2):
            parts.append(rest.astype(BF16))
            rest = rest - parts[-1].astype(F32)
        moved = jnp.dot(jnp.concatenate(parts, axis=0), order_ref[...], preferred_element_type=F32)
        moved = moved[:n] + moved[n:]
        for o in range(p.own):
            mine = moved[o * p.c : (o + 1) * p.c]
            for t in range(p.tiles):
                core = jnp.bitwise_xor(place_ref[0], t % 2)
                chip = t // 2
                block = jnp.concatenate(
                    [mine[f * rows : (f + 1) * rows, t * p.lanes : (t + 1) * p.lanes] for f in range(p.fold)], axis=1
                )
                if chip % 2:
                    odd_ref[chip // 2, core, layer, o] = block
                else:
                    even_refs[chip // 2][core, layer, o] = block


def dual_body(plan, got_ref, *refs):
    p = plan
    place_ref = place_of(p)
    w_refs, cross_ref, out_ref, modes_ref = refs[: p.chips], *refs[p.chips :]
    total = got_ref[0]
    for d in range(1, p.devices):
        total = total + got_ref[d]
    down = total.T
    ks = [down[k * p.c : (k + 1) * p.c, :] for k in range(p.per_row)]
    modes = jnp.concatenate(ks * p.fold, axis=1)
    modes_ref[...] = modes
    rows = p.c // p.fold
    sums = jnp.zeros((rows, LANES), F32)
    for chip in range(p.chips):
        for core in range(2):
            tile = jnp.bitwise_xor(lax.div(place_ref[3], 2), chip) * 2 + jnp.bitwise_xor(place_ref[0], core)
            for o in range(p.own):
                w = cross_ref[chip, o] if core else w_refs[chip][0, o]
                sums = sums + w * modes_ref[pl.ds(tile * p.own + o, 1), :]
    down = sums.T
    pieces = []
    for k in range(p.per_row):
        for f in range(p.fold):
            start = (f * p.per_row + k) * p.slot
            pieces.append(down[start : start + p.slot, :])
    dual = jnp.concatenate(pieces, axis=1)
    parity = place_ref[0]
    for q in range(p.tiles // 2):
        even = modes[2 * q * p.own : (2 * q + 1) * p.own, :]
        odd = modes[(2 * q + 1) * p.own : (2 * q + 2) * p.own, :]
        mine = jnp.where(parity == 0, even, odd)
        other = jnp.where(parity == 0, odd, even)
        pieces = [mine, other]
        if 2 * p.own < SUB:
            pieces.append(jnp.zeros((SUB - 2 * p.own, LANES), F32))
        both = jnp.concatenate(pieces, axis=0)
        for g in range(p.groups):
            d = g * (p.tiles // 2) + q
            out_ref[d, : p.slot, :] = dual
            out_ref[d, p.slot :, :] = both


def grad_body(plan, got_ref, more_ref, saved_ref, out_ref):
    p = plan
    place_ref = place_of(p)
    base = place_ref[1] * (p.tiles // 2)
    parity = place_ref[0]
    lane = lax.broadcasted_iota(jnp.int32, (SUB, LANES), 1)
    source = lane % p.per_row * p.slot + lane % K // p.per_row * p.run + lane // K
    source = jnp.clip(source, 0, LANES - 1)
    pieces = []
    for q in range(p.tiles // 2):
        one = jnp.take_along_axis(got_ref[base + q, p.slot :, :], source, axis=1)[: p.own]
        two = jnp.take_along_axis(more_ref[base + q, p.slot :, :], source, axis=1)[p.own : 2 * p.own]
        for t, piece in (
            (2 * q, jnp.where(parity == 0, one, two)),
            (2 * q + 1, jnp.where(parity == 0, two, one)),
        ):
            if p.valid(t) > 0:
                pieces.append(piece[:, : p.valid(t) * K])
    spectrum = jnp.concatenate(pieces, axis=1)
    for o in range(p.own):
        out_ref[o] = saved_ref[...] * spectrum[o : o + 1, :]


def solution(mesh):
    def local(cotangent, deriv_two, deriv_one, point_two, point_one, modes_two, modes_one, saved_two, saved_one):
        shape = cotangent.shape
        channels = shape[1]
        plan = p = Plan(mesh, shape[2:], channels)
        xy = p.x * p.y

        full_x, full_y, full_z = basis(p.x * p.groups), basis(p.y * p.tiles), basis(p.z)
        rows_x, rows_y = [], []
        for parity in range(2):
            pair, used = [], []
            for h in (parity, 1 - parity):
                for d in range(p.half):
                    tile = d % (p.tiles // 2) * 2 + h
                    own = np.arange(p.run)
                    used.append(own < p.valid(tile))
                    start = d // (p.tiles // 2) * p.pairs + tile * p.run
                    pair.append(np.where(used[-1], start + own, 0))
            pair, used = np.concatenate(pair), np.concatenate(used)
            rows_x.append(full_x[pair // K] * used[:, None].astype(np.float32))
            rows_y.append(full_y[pair % K])
        rows_x = np.stack(rows_x).reshape(2, p.rows, p.groups, p.x).transpose(0, 2, 3, 1)
        rows_x = rows_x.reshape(2 * p.groups, p.x, p.rows)
        rows_y = np.stack(rows_y).reshape(2, p.rows, p.tiles // 2, 2, p.y)
        rows_y = np.stack([rows_y[h, :, :, h] for h in range(2)]).transpose(2, 0, 3, 1)
        rows_y = rows_y.reshape(p.tiles, p.y, p.rows)
        rows_x, rows_y = two_parts(rows_x), two_parts(rows_y)
        ex = jnp.asarray(np.tile(np.repeat(np.eye(p.x, dtype=np.float32), p.y, axis=1), (2, 1))).astype(BF16)
        ey = jnp.asarray(np.tile(np.eye(p.y, dtype=np.float32), (2, p.x))).astype(BF16)
        groups = p.c // p.step
        tz = np.zeros((LANES, p.step, p.z), np.float32)
        lines = np.zeros((K, groups, p.step, groups, LANES), np.float32)
        for u in range(p.step):
            for k in range(K):
                tz[k * p.step + u, u] = full_z[k]
                lines[k, np.arange(groups), u, np.arange(groups), k * p.step + u] = 1.0
        tz = jnp.asarray(tz.reshape(LANES, p.step * p.z)).astype(BF16)
        lines = jnp.asarray(lines.reshape(p.width, groups * LANES)).astype(BF16)
        spread = jnp.asarray(np.repeat(np.eye(p.c, dtype=np.float32), p.y, axis=0)).astype(BF16)

        target = np.full((p.chips, 1, p.tiles * p.lanes), -1, np.int32)
        for chip in range(p.chips):
            for tile in range(p.tiles):
                at = ((tile // 2 ^ chip) * 2 + tile % 2) * p.lanes
                for r in range(p.valid(tile)):
                    for k in range(K):
                        lane = k % p.per_row * p.slot + k // p.per_row * p.run + r
                        target[chip, 0, at + lane] = (tile * p.run + r) * K + k
        target = jnp.asarray(target)

        field = (p.c, xy, p.z)
        slots = (p.devices, p.slot, LANES)
        packed = (p.half, p.packed, LANES)
        g_scr = pltpu.VMEM((groups, xy, LANES), BF16)
        s_scr = pltpu.VMEM((p.rows, p.width), F32)
        modes_scr = g_scr
        blocked = pl.BlockSpec((p.step, xy, p.z), lambda n: (n, 0, 0))
        steps = (p.c // p.step,)
        partners = [(i, i ^ 1) for i in range(p.tiles)]
        same = [
            [e * p.tiles + 2 * q + h for e in range(p.groups) for q in range(p.tiles // 2)] for h in range(2)
        ]

        def in_hbm(array):
            return pltpu.with_memory_space_constraint(array, pltpu.HBM)

        block = (2, 2, p.own, p.c // p.fold, LANES)
        odd, *even = call(
            pack_body, p, [((p.chips // 2, *block), F32)] + [(block, F32)] * (p.chips // 2),
            [
                pltpu.VMEM((p.own, p.c, p.pairs * K), F32),
                pltpu.VMEM((p.own, p.c, p.pairs * K), F32),
                pltpu.VMEM(target.shape, jnp.int32),
                pltpu.VMEM((p.pairs * K, p.tiles * p.lanes), BF16),
                pltpu.SemaphoreType.DMA((3,)),
            ],
            specs=[HBM, HBM, HBM],
        )(in_hbm(modes_two.transpose(1, 2, 0)), in_hbm(modes_one.transpose(1, 2, 0)), in_hbm(target))

        def swap(blocks, bit):
            return lax.ppermute(blocks, "tile", [(i, i ^ (2 * bit)) for i in range(p.tiles)])

        got = swap(odd, 1)
        first = {(0, 2 * n): part for n, part in enumerate(even)}
        first |= {(1, 2 * n): got[n] for n in range(p.chips // 2)}

        def deal(layer):
            held = {key: part[:, layer] for key, part in first.items()}
            bit = 2
            while bit < p.chips:
                leaving = sorted(key for key in held if key[1] & bit)
                parts = jnp.stack([held.pop(key) for key in leaving])
                got = swap(parts, bit)
                held |= {(key[0] ^ bit, key[1] ^ bit): got[n] for n, key in enumerate(leaving)}
                bit *= 2
            dealt = [held[chip, 0] for chip in range(p.chips)]
            crossing = jnp.stack([part[1] for part in dealt])
            return (*dealt, lax.ppermute(crossing, "tile", partners))

        weights_two = deal(0)
        weights_one = deal(1)

        def exchange(parts):
            return lax.all_to_all(parts, BOTH, 0, 0, tiled=True, axis_index_groups=same)

        def partner(parts):
            return lax.ppermute(parts, "tile", partners)

        def dual(got, weights):
            return call(
                dual_body, p, [(packed, F32)], [pltpu.VMEM((p.c, LANES), F32)],
                count=p.chips + 2,
            )(got, *weights)[0]

        def pointwise(w, *factors):
            return call(
                pointwise_body, p, [(field, BF16)], [pltpu.VMEM((p.c * p.y, p.c * p.y), BF16)],
                count=2 + len(factors),
            )(*factors, w, spread)[0]

        def grad(got, more, saved):
            out = call(grad_body, p, [((p.own, p.c, p.pairs * K), F32)], count=3)(got, more, saved[0].T)[0]
            return out.transpose(2, 0, 1)

        part_two, table, turned = call(
            analyse_body, p, [(slots, F32), ((2 * p.rows, xy), BF16), ((xy, p.rows), BF16)],
            [
                g_scr, s_scr, pltpu.VMEM(field, BF16), pltpu.VMEM((2 * p.rows, xy), BF16),
                pltpu.VMEM((xy, p.rows), BF16), pltpu.SemaphoreType.DMA((groups + 2,)),
            ],
            specs=[VMEM, HBM] + [VMEM] * 6, out_specs=[VMEM, HBM, HBM], grid=steps,
        )(cotangent.reshape(field), in_hbm(deriv_two.reshape(field)), tz, lines, rows_x, rows_y, ex, ey)
        got_two = lax.all_to_all(part_two, BOTH, 0, 0, tiled=True)
        point_out = pointwise(point_two, cotangent.reshape(field), deriv_two.reshape(field))
        share_two = dual(got_two, weights_two)
        all_two = exchange(share_two)
        more_two = partner(all_two)
        gated_one, part_one = call(
            synth_analyse_body, p, [(field, BF16), (slots, F32)], [
                g_scr, s_scr, s_scr, modes_scr, pltpu.VMEM(field, BF16), pltpu.SemaphoreType.DMA(steps),
            ],
            count=8, out_specs=[HBM, VMEM], grid=steps,
        )(all_two, more_two, point_out, deriv_one.reshape(field), lines, tz, turned, table)
        got_one = lax.all_to_all(part_one, BOTH, 0, 0, tiled=True)
        grad_two = grad(all_two, more_two, saved_two)
        point_out = pointwise(point_one, gated_one)
        share_one = dual(got_one, weights_one)
        all_one = exchange(share_one)
        more_one = partner(all_one)
        result, grad_one = call(
            synth_body, p, [(field, BF16), ((p.own, p.c, p.pairs * K), F32)],
            [s_scr, modes_scr, pltpu.VMEM((p.own, p.c, p.pairs * K), F32), pltpu.SemaphoreType.DMA((1,))],
            specs=[VMEM] * 7,
            out_specs=[blocked, HBM],
            grid=steps,
        )(all_one, more_one, point_out, tz, lines, turned, saved_one[0].T)
        grad_one = grad_one.transpose(2, 0, 1)
        return (result.reshape(shape), grad_one, grad_two)

    return jax.shard_map(
        local,
        mesh=mesh,
        in_specs=(
            P(None, None, "grp", "tile", None),
            P(None, None, "grp", "tile", None),
            P(None, None, "grp", "tile", None),
            P(),
            P(),
            P("grp", "tile", None),
            P("grp", "tile", None),
            P(None, "grp", None),
            P(None, "grp", None),
        ),
        out_specs=(
            P(None, None, "grp", "tile", None),
            P("grp", "tile", None),
            P("grp", "tile", None),
        ),
        check_vma=False,
    )
```

```python
import functools
import math

import jax
import jax.numpy as jnp
import numpy as np
from jax import lax
from jax.experimental import pallas as pl
from jax.experimental.pallas import tpu as pltpu
from jax.sharding import PartitionSpec as P


K = 12
LANES = 128
SUB = 8
COST = 1 << 31
BOTH = ("grp", "tile")
VMEM = pl.BlockSpec(memory_space=pltpu.VMEM)
HBM = pl.BlockSpec(memory_space=pltpu.HBM)
F32 = jnp.float32
BF16 = jnp.bfloat16


def basis(length):
    position = np.arange(length)
    orders = np.arange(K)
    frequency = (orders + 1) // 2
    phase = frequency[:, None] * position[None, :] % length
    angle = 2.0 * math.pi / length * phase
    factor = math.sqrt(2.0 / length)
    values = np.where(orders[:, None] % 2 == 1, factor * np.cos(angle), factor * np.sin(angle))
    values[0] = 1.0 / math.sqrt(length)
    return values.astype(np.float32)


def place_of(plan):
    group, tile = lax.axis_index("grp"), lax.axis_index("tile")
    parity = jnp.bitwise_and(tile, 1)
    return parity, group, parity * plan.groups + group, tile


def two_parts(table):
    high = table.astype(jnp.bfloat16)
    return jnp.asarray(np.concatenate([high, (table - high.astype(np.float32)).astype(jnp.bfloat16)], axis=1))


class Plan:
    def __init__(self, mesh, cells, channels):
        self.groups, self.tiles = mesh.shape["grp"], mesh.shape["tile"]
        self.devices = self.groups * self.tiles
        self.x, self.y, self.z = cells
        self.c = channels
        self.per_row = LANES // channels
        self.blocks = K // self.per_row
        self.width = K * channels
        self.pairs = K * K // self.groups
        self.run = -(-self.pairs // self.tiles)
        self.slot = -(-self.run * self.blocks // SUB) * SUB
        self.packed = self.slot + SUB
        self.half = self.devices // 2
        self.chips = self.tiles // 2
        self.lanes = self.per_row * self.slot
        self.fold = LANES // self.lanes
        self.rows = self.devices * self.run
        self.own = channels // self.tiles
        self.step = 8

    def valid(self, tile):
        return max(0, min(self.run, self.pairs - self.run * tile))


def call(body, plan, outs, scratch=(), specs=None, out_specs=None, count=None, limit=8, grid=()):
    return pl.pallas_call(
        functools.partial(body, plan),
        grid=grid,
        out_shape=tuple(
            pltpu.HBM(s, d) if spec is not VMEM else jax.ShapeDtypeStruct(s, d)
            for (s, d), spec in zip(outs, out_specs or [VMEM] * len(outs))
        ),
        in_specs=specs or [VMEM] * count,
        out_specs=tuple(out_specs or [VMEM] * len(outs)),
        scratch_shapes=list(scratch),
        compiler_params=pltpu.CompilerParams(vmem_limit_bytes=limit << 20),
        cost_estimate=pl.CostEstimate(flops=COST, bytes_accessed=COST // 1000, transcendentals=0),
    )


def emit_slots(plan, g_ref, order_ref, table_ref, slots_ref, s_ref):
    p = plan
    place_ref = place_of(p)
    lines = jnp.concatenate([g_ref[n] for n in range(p.c // p.step)], axis=1)
    lines = lax.dot_general(lines, order_ref[...], (((1,), (1,)), ((), ())), preferred_element_type=F32).astype(BF16)
    both = jnp.dot(table_ref[...], lines, preferred_element_type=F32)
    s_ref[...] = both[: p.rows] + both[p.rows :]
    for d in range(p.devices):
        parity = place_ref[0] if d < p.half else 1 - place_ref[0]
        n = (d % p.half // p.chips) * p.tiles + d % p.chips * 2 + parity
        for j in range(p.blocks):
            slots_ref[n, j * p.run : (j + 1) * p.run, :] = s_ref[
                d * p.run : (d + 1) * p.run, j * LANES : (j + 1) * LANES
            ]
        if p.blocks * p.run < p.slot:
            slots_ref[n, p.blocks * p.run :, :] = jnp.zeros((p.slot - p.blocks * p.run, LANES), F32)


def product(up, der):
    return (up.astype(F32) * der.astype(F32)).astype(BF16)


def spread_rows(rows, cells):
    return lax.dot_general(rows, cells, (((0,), (0,)), ((), ())), preferred_element_type=F32)


def analyse_body(
    plan, up_ref, der_hbm, tz_ref, order_ref, rx_ref, ry_ref, ex_ref, ey_ref,
    slots_ref, table_hbm, turned_hbm, g_ref, s_ref, der_ref, table_ref, turned_ref, sems,
):
    p = plan
    place_ref = place_of(p)
    step = pl.program_id(0)

    def fetch(n):
        part = pl.ds(n * p.step, p.step)
        return pltpu.make_async_copy(der_hbm.at[part], der_ref.at[part], sems.at[n])

    last = p.c // p.step
    tables = (
        pltpu.make_async_copy(table_ref, table_hbm, sems.at[last]),
        pltpu.make_async_copy(turned_ref, turned_hbm, sems.at[last + 1]),
    )

    @pl.when(step == 0)
    def _():
        for n in range(p.c // p.step):
            fetch(n).start()
        table = spread_rows(rx_ref[place_ref[2]], ex_ref[...]) * spread_rows(ry_ref[place_ref[3]], ey_ref[...])
        high = table.astype(BF16)
        table_ref[: p.rows] = high
        table_ref[p.rows :] = (table - high.astype(F32)).astype(BF16)
        turned_ref[...] = table.T.astype(BF16)
        for copy in tables:
            copy.start()

    first = step * p.step
    fetch(step).wait()
    parts = [product(up_ref[first + u], der_ref[first + u]) for u in range(p.step)]
    g_ref[step] = lax.dot_general(
        jnp.concatenate(parts, axis=1), tz_ref[...], (((1,), (1,)), ((), ())), preferred_element_type=F32
    ).astype(BF16)

    @pl.when(step == pl.num_programs(0) - 1)
    def _():
        emit_slots(p, g_ref, order_ref, table_ref, slots_ref, s_ref)
        for copy in tables:
            copy.wait()


def gather_modes(plan, got_ref, more_ref, order_ref, turned_ref, d_ref, modes_ref):
    p = plan
    for d in range(p.devices):
        from_ref, n = (got_ref, d) if d < p.half else (more_ref, d - p.half)
        for j in range(p.blocks):
            d_ref[d * p.run : (d + 1) * p.run, j * LANES : (j + 1) * LANES] = from_ref[
                n, j * p.run : (j + 1) * p.run, :
            ]
    lines = jnp.dot(turned_ref[...], d_ref[...].astype(BF16), preferred_element_type=F32).astype(BF16)
    lines = jnp.dot(lines, order_ref[...], preferred_element_type=F32).astype(BF16)
    for n in range(p.c // p.step):
        modes_ref[n] = lines[:, n * LANES : (n + 1) * LANES]


def synth_analyse_body(
    plan, got_ref, more_ref, point_ref, der_ref, order_ref, tz_ref, turned_ref, table_ref,
    gated_ref, slots_ref, g_ref, s_ref, d_ref, modes_ref, field_ref, sems,
):
    p = plan
    step = pl.program_id(0)

    def store(n):
        part = pl.ds(n * p.step, p.step)
        return pltpu.make_async_copy(field_ref.at[part], gated_ref.at[part], sems.at[n])

    @pl.when(step == 0)
    def _():
        gather_modes(p, got_ref, more_ref, order_ref, turned_ref, d_ref, modes_ref)

    first = step * p.step
    synth = jnp.dot(modes_ref[step], tz_ref[...], preferred_element_type=F32)
    parts = []
    for u in range(p.step):
        middle = (point_ref[first + u].astype(F32) + synth[:, u * p.z : (u + 1) * p.z]).astype(BF16)
        gated = product(middle, der_ref[first + u])
        field_ref[first + u] = gated
        parts.append(gated)
    store(step).start()
    g_ref[step] = lax.dot_general(
        jnp.concatenate(parts, axis=1), tz_ref[...], (((1,), (1,)), ((), ())), preferred_element_type=F32
    ).astype(BF16)

    @pl.when(step == pl.num_programs(0) - 1)
    def _():
        emit_slots(p, g_ref, order_ref, table_ref, slots_ref, s_ref)
        for n in range(p.c // p.step):
            store(n).wait()


def synth_body(
    plan, got_ref, more_ref, point_ref, tz_ref, order_ref, turned_ref, saved_ref, out_ref, grad_hbm,
    d_ref, modes_ref, grad_ref, sem,
):
    p = plan
    step = pl.program_id(0)
    leaving = pltpu.make_async_copy(grad_ref, grad_hbm, sem.at[0])

    @pl.when(step == 0)
    def _():
        grad_body(p, got_ref, more_ref, saved_ref, grad_ref)
        leaving.start()
        gather_modes(p, got_ref, more_ref, order_ref, turned_ref, d_ref, modes_ref)

    first = step * p.step
    synth = jnp.dot(modes_ref[step], tz_ref[...], preferred_element_type=F32)
    for u in range(p.step):
        out_ref[u] = (point_ref[first + u].astype(F32) + synth[:, u * p.z : (u + 1) * p.z]).astype(BF16)

    @pl.when(step == pl.num_programs(0) - 1)
    def _():
        leaving.wait()


def pointwise_body(plan, *refs):
    p = plan
    *field_refs, w_ref, spread_ref, out_ref, big_ref = refs
    n = p.c * p.y
    spread = spread_ref[...]
    rows = lax.dot_general(spread, w_ref[...], (((1,), (1,)), ((), ())), preferred_element_type=F32).astype(BF16)
    both = lax.dot_general(rows, spread, (((1,), (1,)), ((), ())), preferred_element_type=F32)
    same = (
        lax.broadcasted_iota(jnp.int32, (n, n), 0) % p.y == lax.broadcasted_iota(jnp.int32, (n, n), 1) % p.y
    )
    big_ref[...] = jnp.where(same, both, 0.0).astype(BF16)
    for x in range(0, p.x, 2):
        pair = []
        for h in range(2):
            cells = [ref[:, (x + h) * p.y : (x + h + 1) * p.y, :] for ref in field_refs]
            pair.append((product(*cells) if len(cells) == 2 else cells[0]).reshape(n, p.z))
        out = jnp.dot(big_ref[...], jnp.concatenate(pair, axis=1), preferred_element_type=F32)
        for h in range(2):
            out_ref[:, (x + h) * p.y : (x + h + 1) * p.y, :] = (
                out[:, h * p.z : (h + 1) * p.z].astype(BF16).reshape(p.c, p.y, p.z)
            )


def pack_body(plan, two_hbm, one_hbm, target_hbm, odd_ref, *refs):
    p = plan
    place_ref = place_of(p)
    *even_refs, two_ref, one_ref, target_ref, order_ref, sems = refs
    n = p.own * p.c
    rows = p.c // p.fold
    copies = [
        pltpu.make_async_copy(two_hbm, two_ref, sems.at[0]),
        pltpu.make_async_copy(one_hbm, one_ref, sems.at[1]),
        pltpu.make_async_copy(target_hbm, target_ref, sems.at[2]),
    ]
    for copy in (copies[2], *copies[:2]):
        copy.start()
    copies[2].wait()
    mode = lax.broadcasted_iota(jnp.int32, order_ref.shape, 0)
    order_ref[...] = jnp.where(mode == target_ref[lax.div(place_ref[3], 2)], 1.0, 0.0).astype(BF16)
    for layer, w_ref in enumerate((two_ref, one_ref)):
        copies[layer].wait()
        rest = w_ref[...].reshape(n, p.pairs * K)
        parts = []
        for _ in range(2):
            parts.append(rest.astype(BF16))
            rest = rest - parts[-1].astype(F32)
        moved = jnp.dot(jnp.concatenate(parts, axis=0), order_ref[...], preferred_element_type=F32)
        moved = moved[:n] + moved[n:]
        for o in range(p.own):
            mine = moved[o * p.c : (o + 1) * p.c]
            for t in range(p.tiles):
                core = jnp.bitwise_xor(place_ref[0], t % 2)
                chip = t // 2
                block = jnp.concatenate(
                    [mine[f * rows : (f + 1) * rows, t * p.lanes : (t + 1) * p.lanes] for f in range(p.fold)], axis=1
                )
                if chip % 2:
                    odd_ref[chip // 2, core, layer, o] = block
                else:
                    even_refs[chip // 2][core, layer, o] = block


def dual_body(plan, got_ref, *refs):
    p = plan
    place_ref = place_of(p)
    w_refs, cross_ref, out_ref, modes_ref = refs[: p.chips], *refs[p.chips :]
    sums = [got_ref[d] for d in range(p.devices)]
    while len(sums) > 1:
        sums = [sum(sums[n + 1 : n + 2], sums[n]) for n in range(0, len(sums), 2)]
    total = sums[0]
    down = total.T
    ks = [down[k * p.c : (k + 1) * p.c, :] for k in range(p.per_row)]
    modes = jnp.concatenate(ks * p.fold, axis=1)
    modes_ref[...] = modes
    rows = p.c // p.fold
    sums = jnp.zeros((rows, LANES), F32)
    for chip in range(p.chips):
        for core in range(2):
            tile = jnp.bitwise_xor(lax.div(place_ref[3], 2), chip) * 2 + jnp.bitwise_xor(place_ref[0], core)
            for o in range(p.own):
                w = cross_ref[chip, o] if core else w_refs[chip][0, o]
                sums = sums + w * modes_ref[pl.ds(tile * p.own + o, 1), :]
    down = sums.T
    pieces = []
    for k in range(p.per_row):
        for f in range(p.fold):
            start = (f * p.per_row + k) * p.slot
            pieces.append(down[start : start + p.slot, :])
    dual = jnp.concatenate(pieces, axis=1)
    parity = place_ref[0]
    for q in range(p.tiles // 2):
        even = modes[2 * q * p.own : (2 * q + 1) * p.own, :]
        odd = modes[(2 * q + 1) * p.own : (2 * q + 2) * p.own, :]
        mine = jnp.where(parity == 0, even, odd)
        other = jnp.where(parity == 0, odd, even)
        pieces = [mine, other]
        if 2 * p.own < SUB:
            pieces.append(jnp.zeros((SUB - 2 * p.own, LANES), F32))
        both = jnp.concatenate(pieces, axis=0)
        for g in range(p.groups):
            d = g * (p.tiles // 2) + q
            out_ref[d, : p.slot, :] = dual
            out_ref[d, p.slot :, :] = both


def grad_body(plan, got_ref, more_ref, saved_ref, out_ref):
    p = plan
    place_ref = place_of(p)
    base = place_ref[1] * (p.tiles // 2)
    parity = place_ref[0]
    lane = lax.broadcasted_iota(jnp.int32, (SUB, LANES), 1)
    source = lane % p.per_row * p.slot + lane % K // p.per_row * p.run + lane // K
    source = jnp.clip(source, 0, LANES - 1)
    pieces = []
    for q in range(p.tiles // 2):
        one = jnp.take_along_axis(got_ref[base + q, p.slot :, :], source, axis=1)[: p.own]
        two = jnp.take_along_axis(more_ref[base + q, p.slot :, :], source, axis=1)[p.own : 2 * p.own]
        for t, piece in (
            (2 * q, jnp.where(parity == 0, one, two)),
            (2 * q + 1, jnp.where(parity == 0, two, one)),
        ):
            if p.valid(t) > 0:
                pieces.append(piece[:, : p.valid(t) * K])
    spectrum = jnp.concatenate(pieces, axis=1)
    for o in range(p.own):
        out_ref[o] = saved_ref[...] * spectrum[o : o + 1, :]


def solution(mesh):
    def local(cotangent, deriv_two, deriv_one, point_two, point_one, modes_two, modes_one, saved_two, saved_one):
        shape = cotangent.shape
        channels = shape[1]
        plan = p = Plan(mesh, shape[2:], channels)
        xy = p.x * p.y

        full_x, full_y, full_z = basis(p.x * p.groups), basis(p.y * p.tiles), basis(p.z)
        rows_x, rows_y = [], []
        for parity in range(2):
            pair, used = [], []
            for h in (parity, 1 - parity):
                for d in range(p.half):
                    tile = d % (p.tiles // 2) * 2 + h
                    own = np.arange(p.run)
                    used.append(own < p.valid(tile))
                    start = d // (p.tiles // 2) * p.pairs + tile * p.run
                    pair.append(np.where(used[-1], start + own, 0))
            pair, used = np.concatenate(pair), np.concatenate(used)
            rows_x.append(full_x[pair // K] * used[:, None].astype(np.float32))
            rows_y.append(full_y[pair % K])
        rows_x = np.stack(rows_x).reshape(2, p.rows, p.groups, p.x).transpose(0, 2, 3, 1)
        rows_x = rows_x.reshape(2 * p.groups, p.x, p.rows)
        rows_y = np.stack(rows_y).reshape(2, p.rows, p.tiles // 2, 2, p.y)
        rows_y = np.stack([rows_y[h, :, :, h] for h in range(2)]).transpose(2, 0, 3, 1)
        rows_y = rows_y.reshape(p.tiles, p.y, p.rows)
        rows_x, rows_y = two_parts(rows_x), two_parts(rows_y)
        ex = jnp.asarray(np.tile(np.repeat(np.eye(p.x, dtype=np.float32), p.y, axis=1), (2, 1))).astype(BF16)
        ey = jnp.asarray(np.tile(np.eye(p.y, dtype=np.float32), (2, p.x))).astype(BF16)
        groups = p.c // p.step
        tz = np.zeros((LANES, p.step, p.z), np.float32)
        lines = np.zeros((K, groups, p.step, groups, LANES), np.float32)
        for u in range(p.step):
            for k in range(K):
                tz[k * p.step + u, u] = full_z[k]
                lines[k, np.arange(groups), u, np.arange(groups), k * p.step + u] = 1.0
        tz = jnp.asarray(tz.reshape(LANES, p.step * p.z)).astype(BF16)
        lines = jnp.asarray(lines.reshape(p.width, groups * LANES)).astype(BF16)
        spread = jnp.asarray(np.repeat(np.eye(p.c, dtype=np.float32), p.y, axis=0)).astype(BF16)

        target = np.full((p.chips, 1, p.tiles * p.lanes), -1, np.int32)
        for chip in range(p.chips):
            for tile in range(p.tiles):
                at = ((tile // 2 ^ chip) * 2 + tile % 2) * p.lanes
                for r in range(p.valid(tile)):
                    for k in range(K):
                        lane = k % p.per_row * p.slot + k // p.per_row * p.run + r
                        target[chip, 0, at + lane] = (tile * p.run + r) * K + k
        target = jnp.asarray(target)

        field = (p.c, xy, p.z)
        slots = (p.devices, p.slot, LANES)
        packed = (p.half, p.packed, LANES)
        g_scr = pltpu.VMEM((groups, xy, LANES), BF16)
        s_scr = pltpu.VMEM((p.rows, p.width), F32)
        modes_scr = g_scr
        blocked = pl.BlockSpec((p.step, xy, p.z), lambda n: (n, 0, 0))
        steps = (p.c // p.step,)
        partners = [(i, i ^ 1) for i in range(p.tiles)]
        same = [
            [e * p.tiles + 2 * q + h for e in range(p.groups) for q in range(p.tiles // 2)] for h in range(2)
        ]

        def in_hbm(array):
            return pltpu.with_memory_space_constraint(array, pltpu.HBM)

        block = (2, 2, p.own, p.c // p.fold, LANES)
        odd, *even = call(
            pack_body, p, [((p.chips // 2, *block), F32)] + [(block, F32)] * (p.chips // 2),
            [
                pltpu.VMEM((p.own, p.c, p.pairs * K), F32),
                pltpu.VMEM((p.own, p.c, p.pairs * K), F32),
                pltpu.VMEM(target.shape, jnp.int32),
                pltpu.VMEM((p.pairs * K, p.tiles * p.lanes), BF16),
                pltpu.SemaphoreType.DMA((3,)),
            ],
            specs=[HBM, HBM, HBM],
        )(in_hbm(modes_two.transpose(1, 2, 0)), in_hbm(modes_one.transpose(1, 2, 0)), in_hbm(target))

        def swap(blocks, bit):
            return lax.ppermute(blocks, "tile", [(i, i ^ (2 * bit)) for i in range(p.tiles)])

        got = swap(odd, 1)
        first = {(0, 2 * n): part for n, part in enumerate(even)}
        first |= {(1, 2 * n): got[n] for n in range(p.chips // 2)}

        def deal(layer):
            held = {key: part[:, layer] for key, part in first.items()}
            bit = 2
            while bit < p.chips:
                leaving = sorted(key for key in held if key[1] & bit)
                parts = jnp.stack([held.pop(key) for key in leaving])
                got = swap(parts, bit)
                held |= {(key[0] ^ bit, key[1] ^ bit): got[n] for n, key in enumerate(leaving)}
                bit *= 2
            dealt = [held[chip, 0] for chip in range(p.chips)]
            crossing = jnp.stack([part[1] for part in dealt])
            return (*dealt, lax.ppermute(crossing, "tile", partners))

        weights_two = deal(0)
        weights_one = deal(1)

        def exchange(parts):
            return lax.all_to_all(parts, BOTH, 0, 0, tiled=True, axis_index_groups=same)

        def partner(parts):
            return lax.ppermute(parts, "tile", partners)

        def dual(got, weights):
            return call(
                dual_body, p, [(packed, F32)], [pltpu.VMEM((p.c, LANES), F32)],
                count=p.chips + 2,
            )(got, *weights)[0]

        def pointwise(w, *factors):
            return call(
                pointwise_body, p, [(field, BF16)], [pltpu.VMEM((p.c * p.y, p.c * p.y), BF16)],
                count=2 + len(factors),
            )(*factors, w, spread)[0]

        def grad(got, more, saved):
            out = call(grad_body, p, [((p.own, p.c, p.pairs * K), F32)], count=3)(got, more, saved[0].T)[0]
            return out.transpose(2, 0, 1)

        part_two, table, turned = call(
            analyse_body, p, [(slots, F32), ((2 * p.rows, xy), BF16), ((xy, p.rows), BF16)],
            [
                g_scr, s_scr, pltpu.VMEM(field, BF16), pltpu.VMEM((2 * p.rows, xy), BF16),
                pltpu.VMEM((xy, p.rows), BF16), pltpu.SemaphoreType.DMA((groups + 2,)),
            ],
            specs=[VMEM, HBM] + [VMEM] * 6, out_specs=[VMEM, HBM, HBM], grid=steps,
        )(cotangent.reshape(field), in_hbm(deriv_two.reshape(field)), tz, lines, rows_x, rows_y, ex, ey)
        got_two = lax.all_to_all(part_two, BOTH, 0, 0, tiled=True)
        point_out = pointwise(point_two, cotangent.reshape(field), deriv_two.reshape(field))
        share_two = dual(got_two, weights_two)
        all_two = exchange(share_two)
        more_two = partner(all_two)
        gated_one, part_one = call(
            synth_analyse_body, p, [(field, BF16), (slots, F32)], [
                g_scr, s_scr, s_scr, modes_scr, pltpu.VMEM(field, BF16), pltpu.SemaphoreType.DMA(steps),
            ],
            count=8, out_specs=[HBM, VMEM], grid=steps,
        )(all_two, more_two, point_out, deriv_one.reshape(field), lines, tz, turned, table)
        got_one = lax.all_to_all(part_one, BOTH, 0, 0, tiled=True)
        grad_two = grad(all_two, more_two, saved_two)
        point_out = pointwise(point_one, gated_one)
        share_one = dual(got_one, weights_one)
        all_one = exchange(share_one)
        more_one = partner(all_one)
        result, grad_one = call(
            synth_body, p, [(field, BF16), ((p.own, p.c, p.pairs * K), F32)],
            [s_scr, modes_scr, pltpu.VMEM((p.own, p.c, p.pairs * K), F32), pltpu.SemaphoreType.DMA((1,))],
            specs=[VMEM] * 7,
            out_specs=[blocked, HBM],
            grid=steps,
        )(all_one, more_one, point_out, tz, lines, turned, saved_one[0].T)
        grad_one = grad_one.transpose(2, 0, 1)
        return (result.reshape(shape), grad_one, grad_two)

    return jax.shard_map(
        local,
        mesh=mesh,
        in_specs=(
            P(None, None, "grp", "tile", None),
            P(None, None, "grp", "tile", None),
            P(None, None, "grp", "tile", None),
            P(),
            P(),
            P("grp", "tile", None),
            P("grp", "tile", None),
            P(None, "grp", None),
            P(None, "grp", None),
        ),
        out_specs=(
            P(None, None, "grp", "tile", None),
            P("grp", "tile", None),
            P("grp", "tile", None),
        ),
        check_vma=False,
    )
```
